1024 devices in a mesh: group: 32 (over x, y), dom: 32 (over z, core).
Axes of the slice: x: 4, y: 8, z: 16, core: 2. Of those that a mesh axis runs over, the one named last changes fastest.
Arguments:
- modal_state: float32 [1024, 56, 9, 128], P(('group', 'dom')), may hold values from -6 to 6
- geometry: float32 [1024, 3, 128], P(('group', 'dom')), may hold values from 0.5 to 2
- material: int32 [1024, 128], P(('group', 'dom')), may hold values from 0 to 7
- star_table: float32 [8, 3, 9, 9], replicated, may hold values from -0.75 to 0.75
- flux_table: float32 [8, 2, 9, 9], replicated, may hold values from -0.625 to 0.625
- cohesion: float32 [8], replicated, may hold values from 0.5 to 4
- stiffness: float32 [3, 56, 56], replicated, may hold values from -0.75 to 0.75
- face_project: float32 [4, 21, 56], replicated, may hold values from -0.75 to 0.75
- face_lift: float32 [4, 56, 21], replicated, may hold values from -1.25 to 1.25
- reorient: float32 [3, 21, 21], replicated, may hold values from -1.25 to 1.25
- neighbour_face: int32 [2, 1024, 512], P(None, ('group', 'dom')), may hold values from 0 to 767, as said below
- send_faces: int32 [2, 1024, 4, 64], P(None, ('group', 'dom')), may hold values from 0 to 511
- orientation: int32 [2, 1024, 512], P(None, ('group', 'dom')), may hold values from 0 to 2
- leaving_slots: int32 [1024, 32], P(('group', 'dom')), may hold values from 0 to 127, as said below
- leaving_owner: int32 [1024, 32], P('group'), may hold values from 0 to 31, as said below
Outputs:
- final_state: float32 [1024, 56, 9, 128], P(('group', 'dom'))
The draws below stay inside these ranges and needn't reach their ends.
Inputs may be any that keep to these rules, and one draw needn't show every extreme that they name: `neighbour_face`: entries below 512 name a local trace; entry 512 + m names received trace m; every received trace is named exactly once in each phase and device. `leaving_slots`: each device's entries are distinct and increasing. `leaving_owner`: every device receives exactly 32 elements; at most 2 go from one device to any one device, and in every group some pair reaches 2.
All inputs are finite; a program needn't handle non-finite values.
Results may differ from the reference program's by a relative error of at most 0.0003.
Values sent between devices are 32-bit elements; how exact they have to be, the bound alone decides.
No kernel may reach another device: no remote copies, remote signals or barrier semaphores. Data moves between devices by JAX's collectives and lax.ppermute only.
A program may use at most 128 MiB of HBM per device.

```python
import math
import jax
import jax.numpy as jnp
from jax import lax

MODES = 56
FACE_MODES = 21
FIELDS = 9
TAYLOR = 6
MATS = 8
STEPS_BEFORE = 1
STEPS_AFTER = 1
ELEM = 128
FACE_SLOTS = 64
DEVS = 1024
GROUPS = 32
DOMS = 32
MIG = 32
CAP = 2
FACES = 512


def migration_plan(key):
    root_key = jax.random.fold_in(key, 9137)

    def one_group(group_key):
        key_place, key_offset, key_pick, key_device = jax.random.split(group_key, 4)
        placing = jax.random.permutation(key_place, DOMS).astype(jnp.int32)
        inverse = jnp.zeros((DOMS,), jnp.int32).at[placing].set(jnp.arange(DOMS, dtype=jnp.int32))
        offsets = jax.random.permutation(key_offset, DOMS).astype(jnp.int32)
        chosen = jax.random.permutation(key_pick, 2 * MIG - CAP)[:MIG - CAP].astype(jnp.int32) + CAP
        tokens = jnp.concatenate([jnp.arange(CAP, dtype=jnp.int32), chosen])
        shifts = offsets[tokens // CAP]

        def one_device(device_key, dom_pos):
            key_order, key_slot = jax.random.split(device_key)
            shuffle = jax.random.permutation(key_order, MIG)
            picked = jnp.sort(jax.random.permutation(key_slot, ELEM)[:MIG]).astype(jnp.int32)
            target = (placing[dom_pos] + shifts[shuffle]) % DOMS
            return (picked, inverse[target])
        return jax.vmap(one_device)(jax.random.split(key_device, DOMS), jnp.arange(DOMS, dtype=jnp.int32))
    picked_all, owner_all = jax.vmap(one_group)(jax.random.split(root_key, GROUPS))
    return (picked_all.reshape(DEVS, MIG).astype(jnp.int32), owner_all.reshape(DEVS, MIG).astype(jnp.int32))


def draw_leaving_slots(key, part):
    return migration_plan(key)[0]


def draw_leaving_owner(key, part):
    return migration_plan(key)[1]


def draw_neighbour_face(key, part):

    def one_row(row_key):
        key_order, key_remote, key_inside = jax.random.split(row_key, 3)
        picks = jax.random.permutation(key_order, FACES)
        remote = FACES + jax.random.permutation(key_remote, 4 * FACE_SLOTS).astype(jnp.int32)
        inside = jax.random.randint(key_inside, (FACES,), 0, FACES, dtype=jnp.int32)
        return inside.at[picks[:4 * FACE_SLOTS]].set(remote)
    rows_all = jax.vmap(one_row)(jax.random.split(jax.random.fold_in(key, 5521), 2 * DEVS))
    return rows_all.reshape(2, DEVS, FACES).astype(jnp.int32)


def touch_ends(drawn, stream_key, low, high):
    shape = drawn.shape
    index_at = [jax.random.randint(jax.random.fold_in(stream_key, axis), (), 0, shape[axis]) for axis in range(len(shape))]
    drawn = drawn.at[tuple(index_at)].set(low)
    longest = shape.index(max(shape))
    index_at[longest] = (index_at[longest] + 1) % shape[longest]
    return drawn.at[tuple(index_at)].set(high)


def steps_of(own_key, dims, pieces, smallest, top_value):
    def one(dim, blocks):
        steps = jax.random.uniform(jax.random.fold_in(jax.random.fold_in(own_key, 6), dim), (blocks,), jnp.float32, smallest / len(pieces), top_value / len(pieces))
        return jnp.repeat(jnp.exp(steps), dims[dim] // blocks).reshape((-1,) + (1,) * (len(dims) - dim - 1))

    factor_of = one(*pieces[0])
    for cut in pieces[1:]:
        factor_of = factor_of * one(*cut)
    return factor_of


def gaussian(stream_key, extent, width, most, shards=(), held_as=jnp.bfloat16):
    result = jax.random.normal(stream_key, extent, jnp.float32) * width
    if len(shards) > 0:
        result = steps_of(stream_key, extent, shards, -0.22, 0.18) * result
    return jnp.clip(result, min=-most, max=most).astype(held_as)


def setup_inputs(seed: int = 0) -> dict:
    keys = jax.random.split(jax.random.key(seed), 16)
    return {
        "modal_state": gaussian(keys[0], (DEVS, MODES, FIELDS, ELEM), 1.0, 6.0, ((0, 1024),), jnp.float32),
        "geometry": jnp.clip(jnp.exp(math.log(2.0) - 1.3862944 * jax.random.uniform(keys[1], (DEVS, 3, ELEM), jnp.float32) ** steps_of(keys[1], (DEVS, 3, ELEM), ((0, 1024),), -0.2, 0.2)), 0.5, 2.0),
        "material": touch_ends(jax.random.randint(keys[2], (DEVS, ELEM), 0, MATS), jax.random.fold_in(keys[2], 1), 0, MATS - 1).astype(jnp.int32),
        "star_table": gaussian(keys[3], (MATS, 3, FIELDS, FIELDS), 0.12, 0.75, (), jnp.float32),
        "flux_table": gaussian(keys[4], (MATS, 2, FIELDS, FIELDS), 0.1, 0.625, (), jnp.float32),
        "cohesion": jnp.clip(jnp.exp(jax.random.uniform(keys[5], (MATS,), jnp.float32, math.log(0.5), math.log(4.0))), 0.5, 4.0),
        "stiffness": gaussian(keys[6], (3, MODES, MODES), MODES ** -0.5, 0.75, (), jnp.float32),
        "face_project": gaussian(keys[7], (4, FACE_MODES, MODES), MODES ** -0.5, 0.75, (), jnp.float32),
        "face_lift": gaussian(keys[8], (4, MODES, FACE_MODES), FACE_MODES ** -0.5, 1.25, (), jnp.float32),
        "reorient": gaussian(keys[9], (3, FACE_MODES, FACE_MODES), FACE_MODES ** -0.5, 1.25, (), jnp.float32),
        "neighbour_face": draw_neighbour_face(jax.random.fold_in(keys[15], 71), 0),
        "send_faces": touch_ends(jax.random.randint(keys[11], (2, DEVS, 4, FACE_SLOTS), 0, FACES), jax.random.fold_in(keys[11], 1), 0, FACES - 1).astype(jnp.int32),
        "orientation": touch_ends(jax.random.randint(keys[12], (2, DEVS, FACES), 0, 3), jax.random.fold_in(keys[12], 1), 0, 2).astype(jnp.int32),
        "leaving_slots": draw_leaving_slots(jax.random.fold_in(keys[15], 71), 0),
        "leaving_owner": draw_leaving_owner(jax.random.fold_in(keys[15], 71), 0),
    }


highest = lax.Precision.HIGHEST
friction_coef = 0.6
relax_share = 0.5

def material_ops(material_hot, geometry_now, star_table, flux_table, cohesion):
    kind_count = star_table.shape[0]
    elem_count = material_hot.shape[1]
    star_rows = jnp.dot(star_table.reshape(kind_count, -1).T, material_hot, precision=highest)
    star_rows = (star_rows.reshape(3, -1, elem_count) * geometry_now[:, None, :]).reshape(-1, elem_count)
    flux_rows = jnp.dot(flux_table.reshape(kind_count, -1).T, material_hot, precision=highest)
    yield_row = jnp.dot(cohesion[None, :], material_hot, precision=highest)
    return jnp.concatenate([star_rows, flux_rows, yield_row], axis=0)

def split_ops(element_ops, nfield):
    square = nfield * nfield
    elem_count = element_ops.shape[1]
    star_mix = element_ops[:3 * square].reshape(3, nfield, nfield, elem_count)
    plus_mix = element_ops[3 * square:4 * square].reshape(nfield, nfield, elem_count)
    minus_mix = element_ops[4 * square:5 * square].reshape(nfield, nfield, elem_count)
    return (star_mix, plus_mix, minus_mix, element_ops[5 * square])

def predictor(field_now, star_mix, stiffness):
    mode_count = field_now.shape[0]
    derivative = field_now
    integral = field_now
    factorial = 1.0
    for degree in range(1, TAYLOR):
        summed = jnp.zeros_like(field_now)
        for axis_dim in range(3):
            applied = jnp.dot(stiffness[axis_dim], derivative.reshape(mode_count, -1), precision=highest).reshape(field_now.shape)
            summed = summed + jnp.einsum('mfe,fge->mge', applied, star_mix[axis_dim], precision=highest)
        derivative = -summed
        factorial = factorial * (degree + 1)
        integral = integral + derivative / factorial
    return integral

def volume_term(integral, star_mix, stiffness):
    mode_count = integral.shape[0]
    summed = jnp.zeros_like(integral)
    for axis_dim in range(3):
        applied = jnp.dot(stiffness[axis_dim].T, integral.reshape(mode_count, -1), precision=highest).reshape(integral.shape)
        summed = summed + jnp.einsum('mfe,fge->mge', applied, star_mix[axis_dim], precision=highest)
    return summed

def face_traces(integral, face_project):
    traced = jnp.einsum('ilm,mfe->lfie', face_project, integral, precision=highest)
    return traced.reshape(traced.shape[0] * traced.shape[1], -1)

def flux_term(own_flat, neighbour_flat, orient_row, face_lift, reorient, plus_mix, minus_mix, nfield):
    face_modes = face_lift.shape[2]
    elem_count = plus_mix.shape[2]
    own_trace = own_flat.reshape(face_modes, nfield, 4, elem_count)
    other_trace = neighbour_flat.reshape(face_modes, nfield, 4, elem_count)
    turned = jnp.einsum('hkl,lfie->hkfie', reorient, other_trace, precision=highest)
    choose = (orient_row.reshape(1, 4, elem_count) == jnp.arange(3, dtype=jnp.int32)[:, None, None]).astype(jnp.float32)
    aligned = lax.optimization_barrier(jnp.sum(turned * choose[:, None, None, :, :], axis=0))
    mixed = jnp.einsum('lfie,fge->lgie', own_trace, plus_mix, precision=highest) + jnp.einsum('lfie,fge->lgie', aligned, minus_mix, precision=highest)
    return jnp.einsum('iml,lgie->mge', face_lift, mixed, precision=highest)

def plastic(updated, yield_row):
    stress_zero = updated[0, :6]
    pressure_zero = -(stress_zero[0] + stress_zero[1] + stress_zero[2]) / 3.0
    deviat = stress_zero[:3] + pressure_zero[None, :]
    second = 0.5 * lax.optimization_barrier(jnp.sum(deviat * deviat, axis=0)) + lax.optimization_barrier(jnp.sum(stress_zero[3:6] * stress_zero[3:6], axis=0))
    shear_mag = jnp.sqrt(second)
    yield_stress = yield_row + friction_coef * jnp.maximum(pressure_zero, 0.0)
    factor = 1.0 - relax_share * jnp.maximum(0.0, 1.0 - yield_stress / jnp.maximum(shear_mag, yield_stress))
    pressure = -(updated[:, 0] + updated[:, 1] + updated[:, 2]) / 3.0
    normal = -pressure[:, None, :] + factor[None, None, :] * (updated[:, :3] + pressure[:, None, :])
    shears = factor[None, None, :] * updated[:, 3:6]
    return jnp.concatenate([normal, shears, updated[:, 6:]], axis=1)

def local_update(field_now, element_ops, integral, own_flat, incoming, neighbour_row, orient_row, stiffness, face_lift, reorient):
    nfield = field_now.shape[1]
    star_mix, plus_mix, minus_mix, yield_row = split_ops(element_ops, nfield)
    combined = jnp.concatenate([own_flat, incoming], axis=1)
    neighbour_flat = jnp.take(combined, neighbour_row, axis=1)
    updated = field_now + volume_term(integral, star_mix, stiffness) - flux_term(own_flat, neighbour_flat, orient_row, face_lift, reorient, plus_mix, minus_mix, nfield)
    return plastic(updated, yield_row)

def global_step(state_all, ops_all, phase, neighbour_face, send_faces, orientation, stiffness, face_project, face_lift, reorient):
    nfield = state_all.shape[2]

    def first_half(packed):
        field_now, element_ops, send_row = packed
        star_mix = split_ops(element_ops, nfield)[0]
        integral = predictor(field_now, star_mix, stiffness)
        own_flat = face_traces(integral, face_project)
        outgoing = jnp.take(own_flat, send_row.reshape(-1), axis=1).reshape(own_flat.shape[0], 4, -1)
        return (integral, own_flat, outgoing)
    integ_all, own_all, out_all = lax.map(first_half, (state_all, ops_all, send_faces[phase]))
    trace_rows = out_all.shape[1]
    slot_count = out_all.shape[3]
    grid_view = out_all.reshape(GROUPS, DOMS, trace_rows, 4, slot_count)
    incoming_all = jnp.concatenate([jnp.roll(grid_view[:, :, :, 1], 1, axis=0), jnp.roll(grid_view[:, :, :, 0], -1, axis=0), jnp.roll(grid_view[:, :, :, 3], 1, axis=1), jnp.roll(grid_view[:, :, :, 2], -1, axis=1)], axis=-1).reshape(DEVS, trace_rows, 4 * slot_count)

    def second_half(packed):
        field_now, element_ops, integral, own_flat, received, neighbour_row, orient_row = packed
        return local_update(field_now, element_ops, integral, own_flat, received, neighbour_row, orient_row, stiffness, face_lift, reorient)
    return lax.map(second_half, (state_all, ops_all, integ_all, own_all, incoming_all, neighbour_face[phase], orientation[phase]))

def migrate_rows(rows_all, leaving_slots, leaving_owner):
    dev_count = leaving_slots.shape[0]
    owner_hot = (leaving_owner[:, :, None] == jnp.arange(DOMS, dtype=jnp.int32)[None, None, :]).astype(jnp.int32)
    before = jnp.cumsum(owner_hot, axis=1, dtype=jnp.int32) - owner_hot
    rank_in = lax.optimization_barrier(jnp.sum(before * owner_hot, axis=2, dtype=jnp.int32))
    counts = lax.optimization_barrier(jnp.sum(owner_hot, axis=1, dtype=jnp.int32)).reshape(GROUPS, DOMS, DOMS)
    start_at = (jnp.cumsum(counts, axis=1, dtype=jnp.int32) - counts).reshape(dev_count, DOMS)
    arrival = (jnp.take_along_axis(start_at, leaving_owner, axis=1) + rank_in).astype(jnp.int32)
    dev_ids = jnp.arange(dev_count, dtype=jnp.int32)[:, None]
    new_dev = (dev_ids // DOMS * DOMS + leaving_owner).astype(jnp.int32)
    new_slot = leaving_slots[new_dev, arrival]
    moving = rows_all[dev_ids, :, leaving_slots]
    return rows_all.at[new_dev, :, new_slot].set(moving)

def reference(modal_state, geometry, material, star_table, flux_table, cohesion, stiffness, face_project, face_lift, reorient, neighbour_face, send_faces, orientation, leaving_slots, leaving_owner):
    kind_count = star_table.shape[0]
    material_hot = (material[:, None, :] == jnp.arange(kind_count, dtype=jnp.int32)[None, :, None]).astype(jnp.float32)

    def build_ops(packed):
        return material_ops(packed[0], packed[1], star_table, flux_table, cohesion)
    ops_all = lax.map(build_ops, (material_hot, geometry))
    state_all = modal_state
    for step_index in range(STEPS_BEFORE):
        state_all = global_step(state_all, ops_all, 0, neighbour_face, send_faces, orientation, stiffness, face_project, face_lift, reorient)
    dev_count, mode_count, nfield, elem_count = state_all.shape
    flat_all = migrate_rows(state_all.reshape(dev_count, mode_count * nfield, elem_count), leaving_slots, leaving_owner)
    state_all = flat_all.reshape(dev_count, mode_count, nfield, elem_count)
    desc_all = migrate_rows(jnp.concatenate([geometry, material_hot], axis=1), leaving_slots, leaving_owner)
    ops_all = lax.map(build_ops, (desc_all[:, 3:], desc_all[:, :3]))
    for step_index in range(STEPS_AFTER):
        state_all = global_step(state_all, ops_all, 1, neighbour_face, send_faces, orientation, stiffness, face_project, face_lift, reorient)
    return state_all
```

```python
import functools

import jax
import jax.numpy as jnp
from jax import lax
from jax.experimental import pallas as pl
from jax.experimental.pallas import tpu as pltpu
from jax.sharding import PartitionSpec as P

TAYLOR = 6
FIELDS = 9
LANES = 128
FACE_PAD = 24
TRACE_ROWS = FIELDS * FACE_PAD
MSG_ROWS = 112
STAR_ROWS = 243
OPS_ROWS = 408
VALUES = 512

highest = lax.Precision.HIGHEST
friction_coef = 0.6
relax_share = 0.5
f32 = jnp.float32
bf16 = jnp.bfloat16


def halves(x):
    hi = x.astype(bf16)
    return hi, (x - hi.astype(f32)).astype(bf16)


def left_matrix(a):
    hi, lo = halves(a)
    both = jnp.concatenate([hi.astype(f32), lo.astype(f32)], axis=0).astype(bf16)
    return both, hi


def mm(left, x):
    both, hi = left
    x_hi, x_lo = halves(x)
    rows = hi.shape[0]
    first = jnp.dot(both, x_hi, preferred_element_type=f32)
    return first[:rows] + (first[rows:] + jnp.dot(hi, x_lo, preferred_element_type=f32))


def lane_gather(x, lane):
    return jnp.take_along_axis(x, jnp.broadcast_to(lane, x.shape), axis=1, mode="promise_in_bounds")


def block(f):
    return slice(f * LANES, (f + 1) * LANES)


def spread_rows(ops_ref, first, count, wide_ref):
    for r in range(count):
        wide_ref[r] = jnp.broadcast_to(ops_ref[first + r : first + r + 1, :], (8, LANES))


def mix(load, wide_ref, start, outs):
    accs = [None] * len(outs)
    for f in range(FIELDS):
        value = load(f)
        rows = value.shape[0]
        value = value.reshape(rows // 8, 8, LANES)
        for t, g in enumerate(outs):
            part = value * wide_ref[start + f * FIELDS + g][None]
            accs[t] = part if accs[t] is None else accs[t] + part
    return [a.reshape(-1, LANES) for a in accs]


GROUPS_OF_FIELDS = ((0, 1, 2), (3, 4, 5), (6, 7, 8))


def star_mixed(src_ref, wide_ref, outs):
    load = lambda f: src_ref[:, block(f)]
    parts = []
    for d in range(3):
        parts.append(jnp.concatenate(mix(load, wide_ref, d * 81, outs), axis=1))
    return jnp.concatenate(parts, axis=0)


def first_half_body(place, refs):
    if place:
        (state_ref, recv_ref, qmap_ref, desc_ref, table_ref, send_ref, stiff_ref, project_ref,
         integral_ref, trace_ref, m0, m1, m2, m3, ops_ref, placed_ref,
         wide_ref, deriv_ref) = refs
    else:
        (state_ref, desc_ref, table_ref, send_ref, stiff_ref, project_ref,
         integral_ref, trace_ref, m0, m1, m2, m3, ops_ref, desc_out_ref,
         wide_ref, deriv_ref) = refs
    modes = stiff_ref.shape[0]

    desc = desc_ref[...]
    if place:
        qmap = qmap_ref[...]
        arrives = qmap >= 0
        lane = jnp.maximum(qmap, 0)
        moved = []
        for b in range(4):
            got = recv_ref[pl.ds(b, 64, stride=4), :]
            got = jnp.concatenate([got, got], axis=0)
            moved.append(lane_gather(jnp.transpose(got, (1, 0)), lane))
        moved = jnp.concatenate(moved, axis=0)
        for f in range(FIELDS):
            new = jnp.where(arrives, moved[f * modes : (f + 1) * modes], state_ref[:, block(f)])
            placed_ref[:, block(f)] = new
        desc = jnp.where(arrives, moved[FIELDS * modes :], desc)
        state_now = placed_ref
    else:
        desc_out_ref[...] = desc
        for f in range(FIELDS):
            integral_ref[:, block(f)] = state_ref[f]
        state_now = integral_ref

    kinds = lax.broadcasted_iota(jnp.int32, (8, LANES), 0).astype(f32)
    hot = (jnp.broadcast_to(desc[3:4], (8, LANES)) == kinds).astype(f32)
    rows = jnp.dot(table_ref[...], hot, precision=highest, preferred_element_type=f32)
    row_at = lax.broadcasted_iota(jnp.int32, (OPS_ROWS, LANES), 0)
    scale = jnp.where(
        row_at < 81,
        desc[0:1],
        jnp.where(row_at < 162, desc[1:2], jnp.where(row_at < STAR_ROWS, desc[2:3], 1.0)),
    )
    ops_ref[...] = rows * scale
    spread_rows(ops_ref, 0, STAR_ROWS, wide_ref)

    stiff = left_matrix(-stiff_ref[...])
    deriv_ref[0] = state_now[...]
    if place:
        integral_ref[...] = state_now[...]

    def degree(j, carry):
        coef = carry
        now = deriv_ref.at[lax.rem(j, 2)]
        later = deriv_ref.at[lax.rem(j + 1, 2)]
        for outs in GROUPS_OF_FIELDS:
            new = mm(stiff, star_mixed(now, wide_ref, outs))
            lanes = slice(outs[0] * LANES, (outs[-1] + 1) * LANES)
            later[:, lanes] = new
            integral_ref[:, lanes] = integral_ref[:, lanes] + new * coef
        return coef / (j + 3).astype(f32)

    lax.fori_loop(0, TAYLOR - 1, degree, jnp.float32(0.5))

    project = left_matrix(project_ref[...])
    for outs in GROUPS_OF_FIELDS:
        lanes = slice(outs[0] * LANES, (outs[-1] + 1) * LANES)
        traced = mm(project, integral_ref[:, lanes])
        for t, f in enumerate(outs):
            for i in range(4):
                trace_ref[i, f * FACE_PAD : (f + 1) * FACE_PAD, :] = traced[
                    i * FACE_PAD : (i + 1) * FACE_PAD, block(t)
                ]

    low = lax.broadcasted_iota(jnp.int32, (8, LANES), 1) < 64
    for c, msg_ref in enumerate((m0, m1, m2, m3)):
        index = jnp.broadcast_to(send_ref[c : c + 1, :], (8, LANES))
        lane, face = index & 127, index >> 7
        for r in range(MSG_ROWS // 8):
            out = None
            for i in range(4):
                got = lane_gather(trace_ref[i, r * 8 : r * 8 + 8, :], lane)
                high_row = r * 8 + MSG_ROWS
                if high_row < TRACE_ROWS:
                    other = lane_gather(trace_ref[i, high_row : high_row + 8, :], lane)
                    got = jnp.where(low, got, other)
                out = got if out is None else jnp.where(face == i, got, out)
            msg_ref[r * 8 : r * 8 + 8, :] = out


def middle_body(refs):
    (state_ref, integral_ref, trace_ref, ops_ref, near_ref, volume_ref, own_ref,
     partial_ref, local_ref, wide_ref) = refs
    spread_rows(ops_ref, 0, STAR_ROWS + 81, wide_ref)
    volume = left_matrix(volume_ref[...])
    own = left_matrix(own_ref[...])
    for outs in GROUPS_OF_FIELDS:
        lanes = slice(outs[0] * LANES, (outs[-1] + 1) * LANES)
        load = lambda f: integral_ref[:, block(f)]
        added = mm(volume, star_mixed(integral_ref, wide_ref, outs))
        flux = mm(own, jnp.concatenate(mix(load, wide_ref, STAR_ROWS, outs), axis=1))
        if len(state_ref.shape) == 3:
            before = jnp.concatenate([state_ref[g] for g in outs], axis=1)
        else:
            before = state_ref[:, lanes]
        partial_ref[:, lanes] = before + added - flux
    for i in range(4):
        index = jnp.broadcast_to(near_ref[i : i + 1, :], (8, LANES))
        lane, source = index & 127, index >> 7
        for r in range(TRACE_ROWS // 8):
            rows = slice(r * 8, r * 8 + 8)
            out = None
            for j in range(4):
                got = lane_gather(trace_ref[j, rows, :], lane)
                out = got if out is None else jnp.where(source == j, got, out)
            local_ref[i, rows, :] = out


def last_half_body(pack, refs):
    if pack:
        (partial_ref, local_ref, m0, m1, m2, m3, ops_ref, near_ref, orient_ref, lift_ref,
         desc_ref, src_ref, out_ref, packed_ref, wide_ref, both_ref, turned_ref, sum_ref) = refs
    else:
        (partial_ref, local_ref, m0, m1, m2, m3, ops_ref, near_ref, orient_ref, lift_ref,
         out_ref, wide_ref, both_ref, turned_ref, sum_ref) = refs
    modes = lift_ref.shape[0]
    spread_rows(ops_ref, STAR_ROWS + 81, 81, wide_ref)

    low = lax.broadcasted_iota(jnp.int32, (MSG_ROWS, LANES), 1) < 64
    rest = TRACE_ROWS - MSG_ROWS
    for k, (a, b) in enumerate(((m0, m1), (m2, m3))):
        first, second = a[...], b[...]
        both_ref[k, 0:MSG_ROWS, :] = jnp.where(low, first, pltpu.roll(second, 64, 1))
        upper = jnp.where(low, pltpu.roll(first, 64, 1), second)
        both_ref[k, MSG_ROWS:TRACE_ROWS, :] = upper[:rest]

    for i in range(4):
        index = jnp.broadcast_to(near_ref[i : i + 1, :], (8, LANES))
        lane, source = index & 127, index >> 7
        for r in range(TRACE_ROWS // 8):
            rows = slice(r * 8, r * 8 + 8)
            out = local_ref[i, rows, :]
            for k in range(2):
                out = jnp.where(source == 4 + k, lane_gather(both_ref[k, rows, :], lane), out)
            turned_ref[i, rows, :] = out

    lift = left_matrix(lift_ref[...])
    for outs in GROUPS_OF_FIELDS:
        lanes = slice(outs[0] * LANES, (outs[-1] + 1) * LANES)
        pieces = []
        for i in range(4):
            load = lambda f: turned_ref[i, f * FACE_PAD : (f + 1) * FACE_PAD, :]
            mixed = mix(load, wide_ref, 0, outs)
            orient = jnp.broadcast_to(orient_ref[i : i + 1, :], (FACE_PAD, LANES))
            for h in range(3):
                pieces.append(
                    jnp.concatenate([jnp.where(orient == h, m, 0.0) for m in mixed], axis=1)
                )
        flux = mm(lift, jnp.concatenate(pieces, axis=0))
        wide_out = partial_ref[:, lanes] - flux
        for t, g in enumerate(outs):
            sum_ref[:, block(g)] = wide_out[:, block(t)]

    zero = [sum_ref[0:1, block(f)] for f in range(6)]
    pressure_zero = -(zero[0] + zero[1] + zero[2]) / 3.0
    second = 0.5 * sum((zero[f] + pressure_zero) * (zero[f] + pressure_zero) for f in range(3))
    second = second + sum(zero[f] * zero[f] for f in range(3, 6))
    shear_mag = jnp.sqrt(second)
    yield_row = ops_ref[405:406, :]
    yield_stress = yield_row + friction_coef * jnp.maximum(pressure_zero, 0.0)
    factor = 1.0 - relax_share * jnp.maximum(
        0.0, 1.0 - yield_stress / jnp.maximum(shear_mag, yield_stress)
    )
    normals = [sum_ref[:, block(f)] for f in range(3)]
    pressure = -(normals[0] + normals[1] + normals[2]) / 3.0
    fields = [-pressure + factor * (n + pressure) for n in normals]
    fields += [factor * sum_ref[:, block(f)] for f in range(3, 6)]
    fields += [sum_ref[:, block(f)] for f in range(6, FIELDS)]
    if not pack:
        for f in range(FIELDS):
            out_ref[f] = fields[f]
        return
    for f in range(FIELDS):
        out_ref[:, block(f)] = fields[f]
    values = jnp.concatenate(fields + [desc_ref[...]], axis=0)
    leaving = lane_gather(values, src_ref[...])
    for b in range(4):
        turned = jnp.transpose(leaving[b * LANES : (b + 1) * LANES], (1, 0))
        packed_ref[pl.ds(b, 64, stride=4), :] = turned[:64]


def call(body, outs, scratch, *args):
    return pl.pallas_call(
        lambda *refs: body(refs),
        out_shape=[jax.ShapeDtypeStruct(s, f32) for s in outs],
        in_specs=[pl.BlockSpec(memory_space=pltpu.VMEM)] * len(args),
        out_specs=[pl.BlockSpec(memory_space=pltpu.VMEM)] * len(outs),
        scratch_shapes=[pltpu.VMEM(s, f32) for s in scratch],
        compiler_params=pltpu.CompilerParams(vmem_limit_bytes=48 << 20),
    )(*args)


def exchange(messages):
    out = []
    for axis, (lower, higher) in (("group", messages[:2]), ("dom", messages[2:])):
        size = lax.axis_size(axis)
        up = [(i, (i + 1) % size) for i in range(size)]
        down = [(j, i) for i, j in up]
        out += [lax.ppermute(higher, axis, up), lax.ppermute(lower, axis, down)]
    return out


def migration_maps(own_slots, leaving_owner, elem_count):
    dom_count = lax.axis_size("dom")
    my_dom = lax.axis_index("dom")
    leave_count = own_slots.shape[0]
    capacity = 2 * leave_count // dom_count
    slot_total = capacity * dom_count
    own_owner = lax.dynamic_index_in_dim(leaving_owner, my_dom, 0, keepdims=False)
    order = jnp.arange(leave_count, dtype=jnp.int32)
    slot_ids = jnp.arange(slot_total, dtype=jnp.int32)
    same = (own_owner[None, :] == own_owner[:, None]) & (order[None, :] < order[:, None])
    send_slot = own_owner * capacity + jnp.sum(same.astype(jnp.int32), axis=1)
    source_lane = jnp.sum(
        jnp.where(send_slot[None, :] == slot_ids[:, None], own_slots[None, :], 0), axis=1
    )
    arrivals = jnp.sum((leaving_owner == my_dom).astype(jnp.int32), axis=1)
    doms = jnp.arange(dom_count, dtype=jnp.int32)
    sender, within = slot_ids // capacity, slot_ids % capacity
    ahead = jnp.sum(jnp.where(doms[None, :] < sender[:, None], arrivals[None, :], 0), axis=1)
    mine = jnp.sum(jnp.where(doms[None, :] == sender[:, None], arrivals[None, :], 0), axis=1)
    position = jnp.where(within < mine, ahead + within, -1)
    elems = jnp.arange(elem_count, dtype=jnp.int32)
    rank = (
        jnp.sum(jnp.where(own_slots[:, None] == elems[None, :], order[:, None] + 1, 0), axis=0) - 1
    )
    hit = (position[:, None] == rank[None, :]) & (rank[None, :] >= 0)
    arriving = jnp.sum(jnp.where(hit, slot_ids[:, None] + 1, 0), axis=0) - 1
    source_lane = jnp.concatenate([source_lane, source_lane])
    return source_lane[None, :], arriving[None, :]


def shards(
    modal_state,
    geometry,
    material,
    star_table,
    flux_table,
    cohesion,
    stiffness,
    face_project,
    face_lift,
    reorient,
    neighbour_face,
    send_faces,
    orientation,
    leaving_slots,
    leaving_owner,
):
    modes, nfield, elem_count = modal_state.shape[1:]
    face_modes = face_project.shape[1]
    kinds = star_table.shape[0]
    trace_pad = FACE_PAD - face_modes

    state = jnp.transpose(modal_state[0], (1, 0, 2))
    desc = jnp.concatenate(
        [geometry[0], material[0][None].astype(f32), jnp.zeros((4, elem_count), f32)], axis=0
    )
    table = jnp.concatenate(
        [
            star_table.reshape(kinds, -1),
            flux_table.reshape(kinds, -1),
            cohesion[:, None],
            jnp.zeros((kinds, OPS_ROWS - 406), f32),
        ],
        axis=1,
    ).T
    stiff = jnp.transpose(stiffness, (1, 0, 2)).reshape(modes, 3 * modes)
    volume = jnp.transpose(stiffness, (2, 0, 1)).reshape(modes, 3 * modes)
    project = jnp.pad(face_project, ((0, 0), (0, trace_pad), (0, 0))).reshape(4 * FACE_PAD, modes)
    own = jnp.einsum("iml,iln->mn", face_lift, face_project, precision=highest)
    turned = jnp.einsum("iml,hlk->mihk", face_lift, reorient, precision=highest)
    lift = jnp.pad(turned, ((0, 0), (0, 0), (0, 0), (0, trace_pad))).reshape(modes, -1)

    send = jnp.concatenate([send_faces[:, 0], send_faces[:, 0]], axis=2)
    near = neighbour_face[:, 0].reshape(2, 4, elem_count)
    orient = orientation[:, 0].reshape(2, 4, elem_count)
    source_lane, arriving = migration_maps(leaving_slots[0], leaving_owner, elem_count)

    width = nfield * elem_count
    full = (modes, width)
    traces = (4, TRACE_ROWS, LANES)
    msg = (MSG_ROWS, LANES)
    ops_shape = (OPS_ROWS, LANES)
    wide = (STAR_ROWS, 8, LANES)
    wide_more = (STAR_ROWS + 81, 8, LANES)
    wide_flux = (81, 8, LANES)

    def middle(state_now, integral, trace, ops, phase):
        return call(middle_body, [full, traces], [wide_more],
                    state_now, integral, trace, ops, near[phase], volume, own)

    integral, trace, a, b, c, d, ops, desc = call(
        functools.partial(first_half_body, False),
        [full, traces, msg, msg, msg, msg, ops_shape, (8, LANES)],
        [wide, (2,) + full],
        state, desc, table, send[0], stiff, project,
    )
    incoming = exchange([a, b, c, d])
    partial, local = middle(state, integral, trace, ops, 0)
    stepped, packed = call(
        functools.partial(last_half_body, True),
        [full, (256, LANES)],
        [wide_flux, (2,) + traces[1:], traces, full],
        partial, local, *incoming, ops, near[0], orient[0], lift, desc, source_lane,
    )
    moved = lax.all_to_all(packed, "dom", split_axis=0, concat_axis=0, tiled=True)
    integral, trace, a, b, c, d, ops, placed = call(
        functools.partial(first_half_body, True),
        [full, traces, msg, msg, msg, msg, ops_shape, full],
        [wide, (2,) + full],
        stepped, moved, arriving, desc, table, send[1], stiff, project,
    )
    incoming = exchange([a, b, c, d])
    partial, local = middle(placed, integral, trace, ops, 1)
    (final,) = call(
        functools.partial(last_half_body, False),
        [(nfield, modes, elem_count)],
        [wide_flux, (2,) + traces[1:], traces, full],
        partial, local, *incoming, ops, near[1], orient[1], lift,
    )
    return jnp.transpose(final, (1, 0, 2))[None]


def solution(mesh):
    in_specs = (
        P(("group", "dom"), None, None, None),
        P(("group", "dom"), None, None),
        P(("group", "dom"), None),
        P(),
        P(),
        P(),
        P(),
        P(),
        P(),
        P(),
        P(None, ("group", "dom"), None),
        P(None, ("group", "dom"), None, None),
        P(None, ("group", "dom"), None),
        P(("group", "dom"), None),
        P("group", None),
    )
    out_specs = P(("group", "dom"), None, None, None)
    return jax.shard_map(shards, mesh=mesh, in_specs=in_specs, out_specs=out_specs, check_vma=False)
```

```python
import functools

import jax
import jax.numpy as jnp
from jax import lax
from jax.experimental import pallas as pl
from jax.experimental.pallas import tpu as pltpu
from jax.sharding import PartitionSpec as P

TAYLOR = 6
FIELDS = 9
LANES = 128
FACE_PAD = 24
TRACE_ROWS = FIELDS * FACE_PAD
MSG_ROWS = 112
COEF_PAD = 16
STAR_ROWS = 27 * COEF_PAD
FLUX_ROWS = 18 * COEF_PAD
VALUES = 512

highest = lax.Precision.HIGHEST
friction_coef = 0.6
relax_share = 0.5
f32 = jnp.float32
bf16 = jnp.bfloat16


def halves(x):
    hi = x.astype(bf16)
    return hi, (x - hi.astype(f32)).astype(bf16)


def left_matrix(a):
    hi, lo = halves(a)
    both = jnp.concatenate([hi.astype(f32), lo.astype(f32)], axis=0).astype(bf16)
    return both, hi


def mm(left, x):
    both, hi = left
    x_hi, x_lo = halves(x)
    rows = hi.shape[0]
    first = jnp.dot(both, x_hi, preferred_element_type=f32)
    return first[:rows] + (first[rows:] + jnp.dot(hi, x_lo, preferred_element_type=f32))


def lane_gather(x, lane):
    return jnp.take_along_axis(x, jnp.broadcast_to(lane, x.shape), axis=1, mode="promise_in_bounds")


def block(f):
    return slice(f * LANES, (f + 1) * LANES)


def exact_dot(a, hot):
    total = None
    for _ in range(3):
        part = a.astype(bf16)
        a = a - part.astype(f32)
        term = jnp.dot(part, hot, preferred_element_type=f32)
        total = term if total is None else total + term
    return total


def coefficient_rows(table, hot):
    count = table.shape[0] // 8
    size = -(-table.shape[0] // LANES) * LANES
    wide = jnp.concatenate([table, jnp.zeros((table.shape[0], LANES - FIELDS), f32)], axis=1)
    if size > table.shape[0]:
        wide = jnp.concatenate([wide, jnp.zeros((size - table.shape[0], LANES), f32)], axis=0)
    turned = jnp.transpose(wide, (1, 0))[:COEF_PAD]
    stacked = jnp.concatenate([turned] * count, axis=0)
    pair = lax.broadcasted_iota(jnp.int32, stacked.shape, 0) // COEF_PAD
    at = lax.broadcasted_iota(jnp.int32, stacked.shape, 1) // 8
    many = jnp.concatenate([hot] * (size // 8), axis=0).astype(bf16)
    return exact_dot(jnp.where(pair == at, stacked, 0.0), many)


def spread_rows(ops_ref, first, count, wide_ref, start=0):
    for p in range(count):
        for g in range(FIELDS):
            r = (first + p) * COEF_PAD + g
            wide_ref[start + p * FIELDS + g] = jnp.broadcast_to(ops_ref[r : r + 1, :], (8, LANES))


def mix(load, wide_ref, start, outs):
    accs = [None] * len(outs)
    for f in range(FIELDS):
        value = load(f)
        rows = value.shape[0]
        value = value.reshape(rows // 8, 8, LANES)
        for t, g in enumerate(outs):
            part = value * wide_ref[start + f * FIELDS + g][None]
            accs[t] = part if accs[t] is None else accs[t] + part
    return [a.reshape(-1, LANES) for a in accs]


GROUPS_OF_FIELDS = ((0, 1), (2, 3), (4, 5), (6, 7), (8,))


def star_mixed(src_ref, wide_ref, outs):
    load = lambda f: src_ref[:, block(f)]
    parts = []
    for d in range(3):
        parts.append(jnp.concatenate(mix(load, wide_ref, d * 81, outs), axis=1))
    return jnp.concatenate(parts, axis=0)


def fetch(pairs, sems):
    copies = [pltpu.make_async_copy(a, b, sems.at[n]) for n, (a, b) in enumerate(pairs)]
    for copy in copies:
        copy.start()
    for copy in copies:
        copy.wait()


def one_hot(desc):
    kinds = lax.broadcasted_iota(jnp.int32, (8, LANES), 0).astype(f32)
    return (jnp.broadcast_to(desc[3:4], (8, LANES)) == kinds).astype(f32)


def first_half_body(place, refs):
    phase = 1 if place else 0
    if place:
        (state_ref, recv_ref, maps_ref, desc_ref, star_ref, send_ref, stiff_ref, project_ref,
         integral_ref, trace_ref, m0, m1, m2, m3, ops_ref, hot_ref, placed_ref,
         wide_ref, deriv_ref, padded_ref) = refs
    else:
        (state_in, geometry_in, material_in, star_in, send_in, stiff_in, project_in,
         integral_ref, trace_ref, m0, m1, m2, m3, ops_ref, hot_ref, desc_ref,
         wide_ref, deriv_ref, padded_ref,
         state_ref, geometry_ref, material_ref, star_ref, send_ref, stiff_ref, project_ref,
         sems) = refs
        fetch(
            [(state_in, state_ref), (geometry_in, geometry_ref), (material_in, material_ref),
             (star_in, star_ref), (send_in, send_ref), (stiff_in, stiff_ref),
             (project_in, project_ref)],
            sems,
        )
        desc_ref[...] = jnp.zeros((8, LANES), f32)
        for d in range(3):
            desc_ref[d : d + 1, :] = geometry_ref[d]
        desc_ref[3:4, :] = material_ref[...].astype(f32)
    modes = stiff_ref.shape[1]

    desc = desc_ref[...]
    if place:
        arriving = maps_ref[1:2, :]
        arrives = arriving >= 0
        lane = jnp.maximum(arriving, 0)
        moved = []
        for b in range(4):
            got = recv_ref[pl.ds(b, 64, stride=4), :]
            got = jnp.concatenate([got, got], axis=0)
            moved.append(lane_gather(jnp.transpose(got, (1, 0)), lane))
        moved = jnp.concatenate(moved, axis=0)
        for f in range(FIELDS):
            new = jnp.where(arrives, moved[f * modes : (f + 1) * modes], state_ref[:, block(f)])
            placed_ref[:, block(f)] = new
        desc = jnp.where(arrives, moved[FIELDS * modes :], desc)
        integral_ref[...] = placed_ref[...]
    else:
        for f in range(FIELDS):
            integral_ref[:, block(f)] = state_ref[f]

    hot = one_hot(desc)
    hot_ref[...] = hot
    rows = coefficient_rows(star_ref[...], hot)
    row_at = lax.broadcasted_iota(jnp.int32, (STAR_ROWS, LANES), 0)
    third = STAR_ROWS // 3
    scale = jnp.where(row_at < third, desc[0:1], jnp.where(row_at < 2 * third, desc[1:2], desc[2:3]))
    ops_ref[...] = rows * scale
    spread_rows(ops_ref, 0, 27, wide_ref)

    across = jnp.concatenate([jnp.transpose(stiff_ref[d], (1, 0)) for d in range(3)], axis=0)
    stiff = left_matrix(-jnp.transpose(across, (1, 0)))
    deriv_ref[0] = integral_ref[...]

    def degree(j, coef):
        now = deriv_ref.at[j % 2]
        later = deriv_ref.at[(j + 1) % 2]
        for outs in GROUPS_OF_FIELDS:
            new = mm(stiff, star_mixed(now, wide_ref, outs))
            lanes = slice(outs[0] * LANES, (outs[-1] + 1) * LANES)
            later[:, lanes] = new
            integral_ref[:, lanes] = integral_ref[:, lanes] + new * coef

    coef = 1.0
    for j in range(TAYLOR - 1):
        coef = coef / (j + 2)
        degree(j, coef)

    padded_ref[...] = jnp.zeros(padded_ref.shape, f32)
    for i in range(4):
        padded_ref[i * FACE_PAD : i * FACE_PAD + project_ref.shape[0], :] = project_ref[:, i, :]
    project = left_matrix(padded_ref[...])
    for outs in GROUPS_OF_FIELDS:
        lanes = slice(outs[0] * LANES, (outs[-1] + 1) * LANES)
        traced = mm(project, integral_ref[:, lanes])
        for t, f in enumerate(outs):
            for i in range(4):
                trace_ref[i, f * FACE_PAD : (f + 1) * FACE_PAD, :] = traced[
                    i * FACE_PAD : (i + 1) * FACE_PAD, block(t)
                ]

    low = lax.broadcasted_iota(jnp.int32, (8, LANES), 1) < 64
    for c, msg_ref in enumerate((m0, m1, m2, m3)):
        row = send_ref[phase, 0, c : c + 1, :]
        index = jnp.broadcast_to(jnp.concatenate([row, row], axis=1), (8, LANES))
        lane, face = index & 127, index >> 7
        for r in range(MSG_ROWS // 8):
            out = None
            for i in range(4):
                got = lane_gather(trace_ref[i, r * 8 : r * 8 + 8, :], lane)
                high_row = r * 8 + MSG_ROWS
                if high_row < TRACE_ROWS:
                    other = lane_gather(trace_ref[i, high_row : high_row + 8, :], lane)
                    got = jnp.where(low, got, other)
                out = got if out is None else jnp.where(face == i, got, out)
            msg_ref[r * 8 : r * 8 + 8, :] = out


def to_column(row, size):
    square = (size, row.shape[1])
    diagonal = lax.broadcasted_iota(jnp.int32, square, 0) == lax.broadcasted_iota(
        jnp.int32, square, 1
    )
    return jnp.sum(jnp.where(diagonal, row, 0.0), axis=1, keepdims=True)


def migration_maps(slots, owners, my_dom):
    doms, leave = owners.shape
    capacity = 2 * leave // doms
    total = capacity * doms
    iota = lambda shape, dim: lax.broadcasted_iota(jnp.int32, shape, dim)
    owner = jnp.sum(
        jnp.where(iota(owners.shape, 0) == my_dom, owners, 0).astype(f32), axis=0, keepdims=True
    )
    owner_col = to_column(owner, leave)
    slots_col = to_column(slots.astype(f32), leave)
    square = (leave, leave)
    before = (owner == owner_col) & (iota(square, 1) < iota(square, 0))
    rank = jnp.sum(jnp.where(before, 1.0, 0.0), axis=1, keepdims=True)
    send_slot = owner_col * capacity + rank
    wide = (leave, LANES)
    slot = (iota(wide, 1) % total).astype(f32)
    source = jnp.sum(jnp.where(send_slot == slot, slots_col, 0.0), axis=0, keepdims=True)

    arrivals = jnp.sum(jnp.where(owners == my_dom, 1.0, 0.0), axis=1, keepdims=True)
    wide = (doms, LANES)
    sender = iota(wide, 1) // capacity
    mine = jnp.sum(jnp.where(iota(wide, 0) == sender, arrivals, 0.0), axis=0, keepdims=True)
    ahead = jnp.sum(jnp.where(iota(wide, 0) < sender, arrivals, 0.0), axis=0, keepdims=True)
    lane = iota((1, LANES), 1)
    within = (lane % capacity).astype(f32)
    position = jnp.where((lane < total) & (within < mine), ahead + within, -1.0)
    position_col = to_column(position, LANES)
    wide = (leave, LANES)
    here = slots_col == iota(wide, 1).astype(f32)
    order = iota(wide, 0).astype(f32) + 1.0
    number = jnp.sum(jnp.where(here, order, 0.0), axis=0, keepdims=True) - 1.0
    wide = (LANES, LANES)
    hit = (position_col == number) & (jnp.broadcast_to(number, wide) >= 0.0)
    arriving = jnp.sum(
        jnp.where(hit, iota(wide, 0).astype(f32) + 1.0, 0.0), axis=0, keepdims=True
    )
    return source.astype(jnp.int32), arriving.astype(jnp.int32) - 1


def middle_body(phase, refs):
    (state_ref, integral_ref, trace_ref, ops_ref, hot_ref, near_ref, _, stiff_ref, flux_ref,
     cohesion_ref) = refs[:10]
    if phase == 0:
        (lift_in, project_ref, reorient_ref, slots_ref, owners_ref,
         partial_ref, local_ref, flux_rows_ref, own_ref, lift_ref, maps_ref,
         wide_ref, columns_ref) = refs[10:]
        own_ref[...] = sum(
            jnp.dot(
                jnp.transpose(lift_in[:, i, :], (1, 0)), project_ref[:, i, :],
                precision=highest, preferred_element_type=f32,
            )
            for i in range(4)
        )
        columns_ref[...] = jnp.zeros(columns_ref.shape, f32)
        face_modes = reorient_ref.shape[1]
        for h in range(3):
            back = jnp.transpose(reorient_ref[h], (1, 0))
            for i in range(4):
                at = (i * 3 + h) * FACE_PAD
                columns_ref[at : at + face_modes, :] = jnp.dot(
                    back, lift_in[:, i, :], precision=highest, preferred_element_type=f32
                )
        lift_ref[...] = jnp.transpose(columns_ref[...], (1, 0))
        source, arriving = migration_maps(slots_ref[...], owners_ref[...], lax.axis_index("dom"))
        maps_ref[0:1, :] = source
        maps_ref[1:2, :] = arriving
    else:
        own_ref, partial_ref, local_ref, flux_rows_ref, wide_ref = refs[10:]
    modes = stiff_ref.shape[1]
    hot = hot_ref[...]
    flux_rows_ref[0:FLUX_ROWS, :] = coefficient_rows(flux_ref[...], hot)
    yield_rows = exact_dot(jnp.broadcast_to(cohesion_ref[...], (8, 8)), hot.astype(bf16))
    flux_rows_ref[FLUX_ROWS : FLUX_ROWS + 8, :] = yield_rows
    spread_rows(ops_ref, 0, 27, wide_ref)
    spread_rows(flux_rows_ref, 0, 9, wide_ref, 243)
    volume = left_matrix(jnp.transpose(stiff_ref[...].reshape(3 * modes, modes), (1, 0)))
    own = left_matrix(own_ref[...])
    for outs in GROUPS_OF_FIELDS:
        lanes = slice(outs[0] * LANES, (outs[-1] + 1) * LANES)
        load = lambda f: integral_ref[:, block(f)]
        added = mm(volume, star_mixed(integral_ref, wide_ref, outs))
        flux = mm(own, jnp.concatenate(mix(load, wide_ref, 243, outs), axis=1))
        if len(state_ref.shape) == 3:
            before = jnp.concatenate([state_ref[g] for g in outs], axis=1)
        else:
            before = state_ref[:, lanes]
        partial_ref[:, lanes] = before + added - flux
    for i in range(4):
        index = jnp.broadcast_to(near_ref[phase, :, block(i)], (8, LANES))
        lane, source = index & 127, index >> 7
        for r in range(TRACE_ROWS // 8):
            rows = slice(r * 8, r * 8 + 8)
            out = None
            for j in range(4):
                got = lane_gather(trace_ref[j, rows, :], lane)
                out = got if out is None else jnp.where(source == j, got, out)
            local_ref[i, rows, :] = out


def last_half_body(pack, refs):
    phase = 0 if pack else 1
    if pack:
        (partial_ref, local_ref, m0, m1, m2, m3, ops_ref, near_ref, orient_ref, lift_ref,
         desc_ref, maps_ref, out_ref, packed_ref, wide_ref, both_ref, turned_ref, sum_ref) = refs
    else:
        (partial_ref, local_ref, m0, m1, m2, m3, ops_ref, near_ref, orient_ref, lift_ref,
         out_ref, wide_ref, both_ref, turned_ref, sum_ref) = refs
    modes = lift_ref.shape[0]
    spread_rows(ops_ref, 9, 9, wide_ref)

    low = lax.broadcasted_iota(jnp.int32, (MSG_ROWS, LANES), 1) < 64
    rest = TRACE_ROWS - MSG_ROWS
    for k, (a, b) in enumerate(((m0, m1), (m2, m3))):
        first, second = a[...], b[...]
        both_ref[k, 0:MSG_ROWS, :] = jnp.where(low, first, pltpu.roll(second, 64, 1))
        upper = jnp.where(low, pltpu.roll(first, 64, 1), second)
        both_ref[k, MSG_ROWS:TRACE_ROWS, :] = upper[:rest]

    for i in range(4):
        index = jnp.broadcast_to(near_ref[phase, :, block(i)], (8, LANES))
        lane, source = index & 127, index >> 7
        for r in range(TRACE_ROWS // 8):
            rows = slice(r * 8, r * 8 + 8)
            out = local_ref[i, rows, :]
            for k in range(2):
                out = jnp.where(source == 4 + k, lane_gather(both_ref[k, rows, :], lane), out)
            turned_ref[i, rows, :] = out

    lift = left_matrix(lift_ref[...])
    for outs in GROUPS_OF_FIELDS:
        lanes = slice(outs[0] * LANES, (outs[-1] + 1) * LANES)
        pieces = []
        for i in range(4):
            load = lambda f: turned_ref[i, f * FACE_PAD : (f + 1) * FACE_PAD, :]
            mixed = mix(load, wide_ref, 0, outs)
            orient = jnp.broadcast_to(orient_ref[phase, :, block(i)], (FACE_PAD, LANES))
            for h in range(3):
                pieces.append(
                    jnp.concatenate([jnp.where(orient == h, m, 0.0) for m in mixed], axis=1)
                )
        flux = mm(lift, jnp.concatenate(pieces, axis=0))
        wide_out = partial_ref[:, lanes] - flux
        for t, g in enumerate(outs):
            sum_ref[:, block(g)] = wide_out[:, block(t)]

    zero = [sum_ref[0:1, block(f)] for f in range(6)]
    pressure_zero = -(zero[0] + zero[1] + zero[2]) / 3.0
    second = 0.5 * sum((zero[f] + pressure_zero) * (zero[f] + pressure_zero) for f in range(3))
    second = second + sum(zero[f] * zero[f] for f in range(3, 6))
    shear_mag = jnp.sqrt(second)
    yield_row = ops_ref[FLUX_ROWS : FLUX_ROWS + 1, :]
    yield_stress = yield_row + friction_coef * jnp.maximum(pressure_zero, 0.0)
    factor = 1.0 - relax_share * jnp.maximum(
        0.0, 1.0 - yield_stress / jnp.maximum(shear_mag, yield_stress)
    )
    normals = [sum_ref[:, block(f)] for f in range(3)]
    pressure = -(normals[0] + normals[1] + normals[2]) / 3.0
    fields = [-pressure + factor * (n + pressure) for n in normals]
    fields += [factor * sum_ref[:, block(f)] for f in range(3, 6)]
    fields += [sum_ref[:, block(f)] for f in range(6, FIELDS)]
    if not pack:
        for f in range(FIELDS):
            out_ref[f] = fields[f]
        return
    for f in range(FIELDS):
        out_ref[:, block(f)] = fields[f]
    values = jnp.concatenate(fields + [desc_ref[...]], axis=0)
    leaving = lane_gather(values, maps_ref[0:1, :])
    for b in range(4):
        turned = jnp.transpose(leaving[b * LANES : (b + 1) * LANES], (1, 0))
        packed_ref[pl.ds(b, 64, stride=4), :] = turned[:64]


def call(body, outs, scratch, *args, raw=False):
    space = pltpu.HBM if raw else pltpu.VMEM
    scratch = [pltpu.VMEM(s, f32) for s in scratch]
    if raw:
        scratch += [pltpu.VMEM(a.shape, a.dtype) for a in args]
        scratch += [pltpu.SemaphoreType.DMA((len(args),))]
    outs = [s if isinstance(s, jax.ShapeDtypeStruct) else jax.ShapeDtypeStruct(s, f32) for s in outs]
    return pl.pallas_call(
        lambda *refs: body(refs),
        out_shape=outs,
        in_specs=[pl.BlockSpec(memory_space=space)] * len(args),
        out_specs=[pl.BlockSpec(memory_space=pltpu.VMEM)] * len(outs),
        scratch_shapes=scratch,
        compiler_params=pltpu.CompilerParams(vmem_limit_bytes=48 << 20),
    )(*[pltpu.with_memory_space_constraint(a, pltpu.HBM) for a in args] if raw else args)


def exchange(messages):
    out = []
    for axis, (lower, higher) in (("group", messages[:2]), ("dom", messages[2:])):
        size = lax.axis_size(axis)
        up = [(i, (i + 1) % size) for i in range(size)]
        down = [(j, i) for i, j in up]
        out += [lax.ppermute(higher, axis, up), lax.ppermute(lower, axis, down)]
    return out


def shards(
    modal_state,
    geometry,
    material,
    star_table,
    flux_table,
    cohesion,
    stiffness,
    face_project,
    face_lift,
    reorient,
    neighbour_face,
    send_faces,
    orientation,
    leaving_slots,
    leaving_owner,
):
    modes, nfield, elem_count = modal_state.shape[1:]
    kinds = star_table.shape[0]
    state = jnp.transpose(modal_state[0], (1, 0, 2))
    star = jnp.transpose(star_table, (1, 2, 0, 3)).reshape(3 * nfield * kinds, nfield)
    flux = jnp.transpose(flux_table, (1, 2, 0, 3)).reshape(2 * nfield * kinds, nfield)
    cohesion = cohesion[None, :]
    geometry = jnp.transpose(geometry, (1, 0, 2))
    face_project = jnp.transpose(face_project, (1, 0, 2))
    face_lift = jnp.transpose(face_lift, (2, 0, 1))

    full = (modes, nfield * elem_count)
    traces = (4, TRACE_ROWS, LANES)
    msg = (MSG_ROWS, LANES)
    tile = (8, LANES)
    ops_shape = (STAR_ROWS, LANES)
    flux_shape = (FLUX_ROWS + 8, LANES)
    wide = (243, 8, LANES)
    wide_more = (324, 8, LANES)
    wide_flux = (81, 8, LANES)
    lift_shape = (modes, 12 * FACE_PAD)
    maps_shape = jax.ShapeDtypeStruct((2, LANES), jnp.int32)
    first_scratch = [wide, (2,) + full, (4 * FACE_PAD, modes)]

    integral, trace, a, b, c, d, ops, hot, desc = call(
        functools.partial(first_half_body, False),
        [full, traces, msg, msg, msg, msg, ops_shape, tile, tile],
        first_scratch,
        state, geometry, material, star, send_faces, stiffness, face_project,
        raw=True,
    )
    incoming = exchange([a, b, c, d])
    partial, local, flux_rows, own, lift, maps = call(
        functools.partial(middle_body, 0),
        [full, traces, flux_shape, (modes, modes), lift_shape, maps_shape],
        [wide_more, (12 * FACE_PAD, modes)],
        state, integral, trace, ops, hot, neighbour_face, orientation, stiffness, flux, cohesion,
        face_lift, face_project, reorient, leaving_slots, leaving_owner,
    )
    stepped, packed = call(
        functools.partial(last_half_body, True),
        [full, (256, LANES)],
        [wide_flux, (2,) + traces[1:], traces, full],
        partial, local, *incoming, flux_rows, neighbour_face, orientation, lift, desc, maps,
    )
    moved = lax.all_to_all(packed, "dom", split_axis=0, concat_axis=0, tiled=True)
    integral, trace, a, b, c, d, ops, hot, placed = call(
        functools.partial(first_half_body, True),
        [full, traces, msg, msg, msg, msg, ops_shape, tile, full],
        first_scratch,
        stepped, moved, maps, desc, star, send_faces, stiffness, face_project,
    )
    incoming = exchange([a, b, c, d])
    partial, local, flux_rows = call(
        functools.partial(middle_body, 1),
        [full, traces, flux_shape],
        [wide_more],
        placed, integral, trace, ops, hot, neighbour_face, orientation, stiffness, flux,
        cohesion, own,
    )
    (final,) = call(
        functools.partial(last_half_body, False),
        [(nfield, modes, elem_count)],
        [wide_flux, (2,) + traces[1:], traces, full],
        partial, local, *incoming, flux_rows, neighbour_face, orientation, lift,
    )
    return jnp.transpose(final, (1, 0, 2))[None]


def solution(mesh):
    in_specs = (
        P(("group", "dom"), None, None, None),
        P(("group", "dom"), None, None),
        P(("group", "dom"), None),
        P(),
        P(),
        P(),
        P(),
        P(),
        P(),
        P(),
        P(None, ("group", "dom"), None),
        P(None, ("group", "dom"), None, None),
        P(None, ("group", "dom"), None),
        P(("group", "dom"), None),
        P("group", None),
    )
    out_specs = P(("group", "dom"), None, None, None)
    return jax.shard_map(shards, mesh=mesh, in_specs=in_specs, out_specs=out_specs, check_vma=False)
```

```python
import functools

import jax
import jax.numpy as jnp
from jax import lax
from jax.experimental import pallas as pl
from jax.experimental.pallas import tpu as pltpu
from jax.sharding import PartitionSpec as P

TAYLOR = 6
FIELDS = 9
LANES = 128
FACE_PAD = 24
TRACE_ROWS = FIELDS * FACE_PAD
MSG_ROWS = 112
LATER = 7
COEF_PAD = 16
STAR_ROWS = 27 * COEF_PAD
FLUX_ROWS = 18 * COEF_PAD
VALUES = 512

highest = lax.Precision.HIGHEST
friction_coef = 0.6
relax_share = 0.5
f32 = jnp.float32
bf16 = jnp.bfloat16


def halves(x):
    hi = x.astype(bf16)
    return hi, (x - hi.astype(f32)).astype(bf16)


def left_matrix(a):
    hi, lo = halves(a)
    both = jnp.concatenate([hi.astype(f32), lo.astype(f32)], axis=0).astype(bf16)
    return both, hi


def mm(left, x):
    both, hi = left
    x_hi, x_lo = halves(x)
    rows = hi.shape[0]
    first = jnp.dot(both, x_hi, preferred_element_type=f32)
    return first[:rows] + (first[rows:] + jnp.dot(hi, x_lo, preferred_element_type=f32))


def lane_gather(x, lane):
    return jnp.take_along_axis(x, jnp.broadcast_to(lane, x.shape), axis=1, mode="promise_in_bounds")


def choose(traces, index):
    rows, size = traces.shape
    wide = (size, index.shape[1])
    hot = (lax.broadcasted_iota(jnp.int32, wide, 0) == index).astype(bf16)
    hi, lo = halves(traces)
    return jnp.dot(hi, hot, preferred_element_type=f32) + jnp.dot(
        lo, hot, preferred_element_type=f32
    )


def block(f):
    return slice(f * LANES, (f + 1) * LANES)


def exact_dot(a, hot):
    total = None
    for _ in range(3):
        part = a.astype(bf16)
        a = a - part.astype(f32)
        term = jnp.dot(part, hot, preferred_element_type=f32)
        total = term if total is None else total + term
    return total


def coefficient_rows(table, hot):
    count = table.shape[0] // 8
    size = -(-table.shape[0] // LANES) * LANES
    wide = jnp.concatenate([table, jnp.zeros((table.shape[0], LANES - FIELDS), f32)], axis=1)
    if size > table.shape[0]:
        wide = jnp.concatenate([wide, jnp.zeros((size - table.shape[0], LANES), f32)], axis=0)
    turned = jnp.transpose(wide, (1, 0))[:COEF_PAD]
    stacked = jnp.concatenate([turned] * count, axis=0)
    pair = lax.broadcasted_iota(jnp.int32, stacked.shape, 0) // COEF_PAD
    at = lax.broadcasted_iota(jnp.int32, stacked.shape, 1) // 8
    many = jnp.concatenate([hot] * (size // 8), axis=0).astype(bf16)
    return exact_dot(jnp.where(pair == at, stacked, 0.0), many)


def spread_rows(ops_ref, first, count, wide_ref, start=0):
    for p in range(count):
        for g in range(FIELDS):
            r = (first + p) * COEF_PAD + g
            wide_ref[start + p * FIELDS + g] = jnp.broadcast_to(ops_ref[r : r + 1, :], (8, LANES))


def mix(load, wide_ref, start, outs):
    accs = [None] * len(outs)
    for f in range(FIELDS):
        value = load(f)
        rows = value.shape[0]
        value = value.reshape(rows // 8, 8, LANES)
        for t, g in enumerate(outs):
            part = value * wide_ref[start + f * FIELDS + g][None]
            accs[t] = part if accs[t] is None else accs[t] + part
    return [a.reshape(-1, LANES) for a in accs]


GROUPS_OF_FIELDS = ((0, 1), (2, 3), (4, 5), (6, 7), (8,))


def star_mixed(src_ref, wide_ref, outs):
    load = lambda f: src_ref[:, block(f)]
    parts = []
    for d in range(3):
        parts.append(jnp.concatenate(mix(load, wide_ref, d * 81, outs), axis=1))
    return jnp.concatenate(parts, axis=0)


def fetch(pairs, sems):
    copies = [pltpu.make_async_copy(a, b, sems.at[n]) for n, (a, b) in enumerate(pairs)]
    for copy in copies:
        copy.start()
    return copies


def one_hot(desc):
    kinds = lax.broadcasted_iota(jnp.int32, (8, LANES), 0).astype(f32)
    return (jnp.broadcast_to(desc[3:4], (8, LANES)) == kinds).astype(f32)


def first_half_body(place, refs):
    phase = 1 if place else 0
    if place:
        (state_ref, recv_ref, maps_ref, desc_ref, star_ref, send_ref, stiff_ref, project_ref,
         integral_ref, trace_ref, m0, m1, m2, m3, ops_ref, hot_ref, placed_ref,
         wide_ref, deriv_ref, padded_ref) = refs
    else:
        count = 7 + LATER
        inputs, refs = refs[:count], refs[count:]
        (integral_ref, trace_ref, m0, m1, m2, m3, ops_ref, hot_ref, desc_ref) = refs[:9]
        held = refs[9 : 14 + LATER]
        state_ref, star_ref, send_ref, stiff_ref, project_ref = held[:5]
        (wide_ref, deriv_ref, padded_ref, geometry_ref, material_ref, sems) = refs[14 + LATER :]
        targets = [geometry_ref, material_ref] + list(held)
        copies = fetch(list(zip(inputs, targets)), sems)
        for copy in copies[:7]:
            copy.wait()
        desc_ref[...] = jnp.zeros((8, LANES), f32)
        for d in range(3):
            desc_ref[d : d + 1, :] = geometry_ref[d]
        desc_ref[3:4, :] = material_ref[...].astype(f32)
    modes = stiff_ref.shape[1]

    desc = desc_ref[...]
    if place:
        arriving = maps_ref[1:2, :]
        arrives = arriving >= 0
        lane = jnp.maximum(arriving, 0)
        moved = []
        for b in range(4):
            got = recv_ref[pl.ds(b, 64, stride=4), :]
            got = jnp.concatenate([got, got], axis=0)
            moved.append(lane_gather(jnp.transpose(got, (1, 0)), lane))
        moved = jnp.concatenate(moved, axis=0)
        for f in range(FIELDS):
            new = jnp.where(arrives, moved[f * modes : (f + 1) * modes], state_ref[:, block(f)])
            placed_ref[:, block(f)] = new
        desc = jnp.where(arrives, moved[FIELDS * modes :], desc)
        integral_ref[...] = placed_ref[...]
    else:
        for f in range(FIELDS):
            integral_ref[:, block(f)] = state_ref[f]

    hot = one_hot(desc)
    hot_ref[...] = hot
    rows = coefficient_rows(star_ref[...], hot)
    row_at = lax.broadcasted_iota(jnp.int32, (STAR_ROWS, LANES), 0)
    third = STAR_ROWS // 3
    scale = jnp.where(row_at < third, desc[0:1], jnp.where(row_at < 2 * third, desc[1:2], desc[2:3]))
    ops_ref[...] = rows * scale
    spread_rows(ops_ref, 0, 27, wide_ref)

    across = jnp.concatenate([jnp.transpose(stiff_ref[d], (1, 0)) for d in range(3)], axis=0)
    stiff = left_matrix(-jnp.transpose(across, (1, 0)))
    deriv_ref[0] = integral_ref[...]

    def degree(j, coef):
        now = deriv_ref.at[j % 2]
        later = deriv_ref.at[(j + 1) % 2]
        for outs in GROUPS_OF_FIELDS:
            new = mm(stiff, star_mixed(now, wide_ref, outs))
            lanes = slice(outs[0] * LANES, (outs[-1] + 1) * LANES)
            later[:, lanes] = new
            integral_ref[:, lanes] = integral_ref[:, lanes] + new * coef

    coef = 1.0
    for j in range(TAYLOR - 1):
        coef = coef / (j + 2)
        degree(j, coef)

    padded_ref[...] = jnp.zeros(padded_ref.shape, f32)
    for i in range(4):
        padded_ref[i * FACE_PAD : i * FACE_PAD + project_ref.shape[0], :] = project_ref[:, i, :]
    project = left_matrix(padded_ref[...])
    for outs in GROUPS_OF_FIELDS:
        lanes = slice(outs[0] * LANES, (outs[-1] + 1) * LANES)
        traced = mm(project, integral_ref[:, lanes])
        for t, f in enumerate(outs):
            for i in range(4):
                trace_ref[i, f * FACE_PAD : (f + 1) * FACE_PAD, :] = traced[
                    i * FACE_PAD : (i + 1) * FACE_PAD, block(t)
                ]

    traces = jnp.concatenate([trace_ref[i] for i in range(4)], axis=1)
    low = lax.broadcasted_iota(jnp.int32, (MSG_ROWS, LANES), 1) < 64
    fill = jnp.zeros((2 * MSG_ROWS - TRACE_ROWS, LANES), f32)
    for k, (a, b) in enumerate(((m0, m1), (m2, m3))):
        pair = [send_ref[phase, 0, c : c + 1, :] for c in (2 * k, 2 * k + 1)]
        sent = choose(traces, jnp.concatenate(pair, axis=1))
        upper = jnp.concatenate([sent[MSG_ROWS:], fill], axis=0)
        a[...] = jnp.where(low, sent[:MSG_ROWS], pltpu.roll(upper, 64, 1))
        b[...] = jnp.where(low, pltpu.roll(sent[:MSG_ROWS], 64, 1), upper)
    if not place:
        for copy in copies[7:]:
            copy.wait()


def to_column(row, size):
    square = (size, row.shape[1])
    diagonal = lax.broadcasted_iota(jnp.int32, square, 0) == lax.broadcasted_iota(
        jnp.int32, square, 1
    )
    return jnp.sum(jnp.where(diagonal, row, 0.0), axis=1, keepdims=True)


def migration_maps(slots, owners, my_dom):
    doms, leave = owners.shape
    capacity = 2 * leave // doms
    total = capacity * doms
    iota = lambda shape, dim: lax.broadcasted_iota(jnp.int32, shape, dim)
    owner = jnp.sum(
        jnp.where(iota(owners.shape, 0) == my_dom, owners, 0).astype(f32), axis=0, keepdims=True
    )
    owner_col = to_column(owner, leave)
    slots_col = to_column(slots.astype(f32), leave)
    square = (leave, leave)
    before = (owner == owner_col) & (iota(square, 1) < iota(square, 0))
    rank = jnp.sum(jnp.where(before, 1.0, 0.0), axis=1, keepdims=True)
    send_slot = owner_col * capacity + rank
    wide = (leave, LANES)
    slot = (iota(wide, 1) % total).astype(f32)
    source = jnp.sum(jnp.where(send_slot == slot, slots_col, 0.0), axis=0, keepdims=True)

    arrivals = jnp.sum(jnp.where(owners == my_dom, 1.0, 0.0), axis=1, keepdims=True)
    wide = (doms, LANES)
    sender = iota(wide, 1) // capacity
    mine = jnp.sum(jnp.where(iota(wide, 0) == sender, arrivals, 0.0), axis=0, keepdims=True)
    ahead = jnp.sum(jnp.where(iota(wide, 0) < sender, arrivals, 0.0), axis=0, keepdims=True)
    lane = iota((1, LANES), 1)
    within = (lane % capacity).astype(f32)
    position = jnp.where((lane < total) & (within < mine), ahead + within, -1.0)
    position_col = to_column(position, LANES)
    wide = (leave, LANES)
    here = slots_col == iota(wide, 1).astype(f32)
    order = iota(wide, 0).astype(f32) + 1.0
    number = jnp.sum(jnp.where(here, order, 0.0), axis=0, keepdims=True) - 1.0
    wide = (LANES, LANES)
    hit = (position_col == number) & (jnp.broadcast_to(number, wide) >= 0.0)
    arriving = jnp.sum(
        jnp.where(hit, iota(wide, 0).astype(f32) + 1.0, 0.0), axis=0, keepdims=True
    )
    return source.astype(jnp.int32), arriving.astype(jnp.int32) - 1


def middle_body(phase, refs):
    (state_ref, integral_ref, trace_ref, ops_ref, hot_ref, near_ref, _, stiff_ref, flux_ref,
     cohesion_ref) = refs[:10]
    if phase == 0:
        (lift_in, project_ref, reorient_ref, slots_ref, owners_ref,
         partial_ref, local_ref, flux_rows_ref, own_ref, lift_ref, maps_ref,
         wide_ref, columns_ref) = refs[10:]
        own_ref[...] = sum(
            jnp.dot(
                jnp.transpose(lift_in[:, i, :], (1, 0)), project_ref[:, i, :],
                precision=highest, preferred_element_type=f32,
            )
            for i in range(4)
        )
        columns_ref[...] = jnp.zeros(columns_ref.shape, f32)
        face_modes = reorient_ref.shape[1]
        for h in range(3):
            back = jnp.transpose(reorient_ref[h], (1, 0))
            for i in range(4):
                at = (i * 3 + h) * FACE_PAD
                columns_ref[at : at + face_modes, :] = jnp.dot(
                    back, lift_in[:, i, :], precision=highest, preferred_element_type=f32
                )
        lift_ref[...] = jnp.transpose(columns_ref[...], (1, 0))
        source, arriving = migration_maps(slots_ref[...], owners_ref[...], lax.axis_index("dom"))
        maps_ref[0:1, :] = source
        maps_ref[1:2, :] = arriving
    else:
        own_ref, partial_ref, local_ref, flux_rows_ref, wide_ref = refs[10:]
    modes = stiff_ref.shape[1]
    hot = hot_ref[...]
    flux_rows_ref[0:FLUX_ROWS, :] = coefficient_rows(flux_ref[...], hot)
    yield_rows = exact_dot(jnp.broadcast_to(cohesion_ref[...], (8, 8)), hot.astype(bf16))
    flux_rows_ref[FLUX_ROWS : FLUX_ROWS + 8, :] = yield_rows
    spread_rows(ops_ref, 0, 27, wide_ref)
    spread_rows(flux_rows_ref, 0, 9, wide_ref, 243)
    volume = left_matrix(jnp.transpose(stiff_ref[...].reshape(3 * modes, modes), (1, 0)))
    own = left_matrix(own_ref[...])
    for outs in GROUPS_OF_FIELDS:
        lanes = slice(outs[0] * LANES, (outs[-1] + 1) * LANES)
        load = lambda f: integral_ref[:, block(f)]
        added = mm(volume, star_mixed(integral_ref, wide_ref, outs))
        flux = mm(own, jnp.concatenate(mix(load, wide_ref, 243, outs), axis=1))
        if len(state_ref.shape) == 3:
            before = jnp.concatenate([state_ref[g] for g in outs], axis=1)
        else:
            before = state_ref[:, lanes]
        partial_ref[:, lanes] = before + added - flux
    for i in range(4):
        index = jnp.broadcast_to(near_ref[phase, :, block(i)], (8, LANES))
        lane, source = index & 127, index >> 7
        for r in range(TRACE_ROWS // 8):
            rows = slice(r * 8, r * 8 + 8)
            out = None
            for j in range(4):
                got = lane_gather(trace_ref[j, rows, :], lane)
                out = got if out is None else jnp.where(source == j, got, out)
            local_ref[i, rows, :] = out


def last_half_body(pack, refs):
    phase = 0 if pack else 1
    if pack:
        (partial_ref, local_ref, m0, m1, m2, m3, ops_ref, near_ref, orient_ref, lift_ref,
         desc_ref, maps_ref, out_ref, packed_ref, wide_ref, both_ref, turned_ref, sum_ref) = refs
    else:
        (partial_ref, local_ref, m0, m1, m2, m3, ops_ref, near_ref, orient_ref, lift_ref,
         out_ref, wide_ref, both_ref, turned_ref, sum_ref) = refs
    modes = lift_ref.shape[0]
    spread_rows(ops_ref, 9, 9, wide_ref)

    low = lax.broadcasted_iota(jnp.int32, (MSG_ROWS, LANES), 1) < 64
    rest = TRACE_ROWS - MSG_ROWS
    for k, (a, b) in enumerate(((m0, m1), (m2, m3))):
        first, second = a[...], b[...]
        both_ref[k, 0:MSG_ROWS, :] = jnp.where(low, first, pltpu.roll(second, 64, 1))
        upper = jnp.where(low, pltpu.roll(first, 64, 1), second)
        both_ref[k, MSG_ROWS:TRACE_ROWS, :] = upper[:rest]

    for i in range(4):
        index = jnp.broadcast_to(near_ref[phase, :, block(i)], (8, LANES))
        lane, source = index & 127, index >> 7
        for r in range(TRACE_ROWS // 8):
            rows = slice(r * 8, r * 8 + 8)
            out = local_ref[i, rows, :]
            for k in range(2):
                out = jnp.where(source == 4 + k, lane_gather(both_ref[k, rows, :], lane), out)
            turned_ref[i, rows, :] = out

    lift = left_matrix(lift_ref[...])
    for outs in GROUPS_OF_FIELDS:
        lanes = slice(outs[0] * LANES, (outs[-1] + 1) * LANES)
        pieces = []
        for i in range(4):
            load = lambda f: turned_ref[i, f * FACE_PAD : (f + 1) * FACE_PAD, :]
            mixed = mix(load, wide_ref, 0, outs)
            orient = jnp.broadcast_to(orient_ref[phase, :, block(i)], (FACE_PAD, LANES))
            for h in range(3):
                pieces.append(
                    jnp.concatenate([jnp.where(orient == h, m, 0.0) for m in mixed], axis=1)
                )
        flux = mm(lift, jnp.concatenate(pieces, axis=0))
        wide_out = partial_ref[:, lanes] - flux
        for t, g in enumerate(outs):
            sum_ref[:, block(g)] = wide_out[:, block(t)]

    zero = [sum_ref[0:1, block(f)] for f in range(6)]
    pressure_zero = -(zero[0] + zero[1] + zero[2]) / 3.0
    second = 0.5 * sum((zero[f] + pressure_zero) * (zero[f] + pressure_zero) for f in range(3))
    second = second + sum(zero[f] * zero[f] for f in range(3, 6))
    shear_mag = jnp.sqrt(second)
    yield_row = ops_ref[FLUX_ROWS : FLUX_ROWS + 1, :]
    yield_stress = yield_row + friction_coef * jnp.maximum(pressure_zero, 0.0)
    factor = 1.0 - relax_share * jnp.maximum(
        0.0, 1.0 - yield_stress / jnp.maximum(shear_mag, yield_stress)
    )
    normals = [sum_ref[:, block(f)] for f in range(3)]
    pressure = -(normals[0] + normals[1] + normals[2]) / 3.0
    fields = [-pressure + factor * (n + pressure) for n in normals]
    fields += [factor * sum_ref[:, block(f)] for f in range(3, 6)]
    fields += [sum_ref[:, block(f)] for f in range(6, FIELDS)]
    if not pack:
        for f in range(FIELDS):
            out_ref[f] = fields[f]
        return
    for f in range(FIELDS):
        out_ref[:, block(f)] = fields[f]
    values = jnp.concatenate(fields + [desc_ref[...]], axis=0)
    leaving = lane_gather(values, maps_ref[0:1, :])
    for b in range(4):
        turned = jnp.transpose(leaving[b * LANES : (b + 1) * LANES], (1, 0))
        packed_ref[pl.ds(b, 64, stride=4), :] = turned[:64]


def call(body, outs, scratch, *args, raw=False):
    space = pltpu.HBM if raw else pltpu.VMEM
    scratch = [s if not isinstance(s, tuple) else pltpu.VMEM(s, f32) for s in scratch]
    outs = [s if isinstance(s, jax.ShapeDtypeStruct) else jax.ShapeDtypeStruct(s, f32) for s in outs]
    return pl.pallas_call(
        lambda *refs: body(refs),
        out_shape=outs,
        in_specs=[pl.BlockSpec(memory_space=space)] * len(args),
        out_specs=[pl.BlockSpec(memory_space=pltpu.VMEM)] * len(outs),
        scratch_shapes=scratch,
        compiler_params=pltpu.CompilerParams(vmem_limit_bytes=48 << 20),
    )(*[pltpu.with_memory_space_constraint(a, pltpu.HBM) for a in args] if raw else args)


def exchange(messages):
    out = []
    for axis, (lower, higher) in (("group", messages[:2]), ("dom", messages[2:])):
        size = lax.axis_size(axis)
        up = [(i, (i + 1) % size) for i in range(size)]
        down = [(j, i) for i, j in up]
        out += [lax.ppermute(higher, axis, up), lax.ppermute(lower, axis, down)]
    return out


def shards(
    modal_state,
    geometry,
    material,
    star_table,
    flux_table,
    cohesion,
    stiffness,
    face_project,
    face_lift,
    reorient,
    neighbour_face,
    send_faces,
    orientation,
    leaving_slots,
    leaving_owner,
):
    modes, nfield, elem_count = modal_state.shape[1:]
    kinds = star_table.shape[0]
    state = jnp.transpose(modal_state[0], (1, 0, 2))
    star = jnp.transpose(star_table, (1, 2, 0, 3)).reshape(3 * nfield * kinds, nfield)
    flux = jnp.transpose(flux_table, (1, 2, 0, 3)).reshape(2 * nfield * kinds, nfield)
    cohesion = cohesion[None, :]
    geometry = jnp.transpose(geometry, (1, 0, 2))
    face_project = jnp.transpose(face_project, (1, 0, 2))
    face_lift = jnp.transpose(face_lift, (2, 0, 1))

    full = (modes, nfield * elem_count)
    traces = (4, TRACE_ROWS, LANES)
    msg = (MSG_ROWS, LANES)
    tile = (8, LANES)
    ops_shape = (STAR_ROWS, LANES)
    flux_shape = (FLUX_ROWS + 8, LANES)
    wide = (243, 8, LANES)
    wide_more = (324, 8, LANES)
    wide_flux = (81, 8, LANES)
    lift_shape = (modes, 12 * FACE_PAD)
    maps_shape = jax.ShapeDtypeStruct((2, LANES), jnp.int32)
    first_scratch = [wide, (2,) + full, (4 * FACE_PAD, modes)]

    kept = [state, star, send_faces, stiffness, face_project,
            face_lift, reorient, leaving_slots, leaving_owner, neighbour_face, orientation, cohesion]
    (integral, trace, a, b, c, d, ops, hot, desc,
     state, star, sends, stiff, project, *later) = call(
        functools.partial(first_half_body, False),
        [full, traces, msg, msg, msg, msg, ops_shape, tile, tile]
        + [jax.ShapeDtypeStruct(a.shape, a.dtype) for a in kept],
        first_scratch
        + [pltpu.VMEM(geometry.shape, f32), pltpu.VMEM(material.shape, jnp.int32),
           pltpu.SemaphoreType.DMA((2 + len(kept),))],
        geometry, material, *kept,
        raw=True,
    )
    face_lift, reorient, slots, owners, near, orient, cohesion = later
    incoming = exchange([a, b, c, d])
    partial, local, flux_rows, own, lift, maps = call(
        functools.partial(middle_body, 0),
        [full, traces, flux_shape, (modes, modes), lift_shape, maps_shape],
        [wide_more, (12 * FACE_PAD, modes)],
        state, integral, trace, ops, hot, near, orient, stiff, flux, cohesion,
        face_lift, project, reorient, slots, owners,
    )
    stepped, packed = call(
        functools.partial(last_half_body, True),
        [full, (256, LANES)],
        [wide_flux, (2,) + traces[1:], traces, full],
        partial, local, *incoming, flux_rows, near, orient, lift, desc, maps,
    )
    moved = lax.all_to_all(packed, "dom", split_axis=0, concat_axis=0, tiled=True)
    integral, trace, a, b, c, d, ops, hot, placed = call(
        functools.partial(first_half_body, True),
        [full, traces, msg, msg, msg, msg, ops_shape, tile, full],
        first_scratch,
        stepped, moved, maps, desc, star, sends, stiff, project,
    )
    incoming = exchange([a, b, c, d])
    partial, local, flux_rows = call(
        functools.partial(middle_body, 1),
        [full, traces, flux_shape],
        [wide_more],
        placed, integral, trace, ops, hot, near, orient, stiff, flux,
        cohesion, own,
    )
    (final,) = call(
        functools.partial(last_half_body, False),
        [(nfield, modes, elem_count)],
        [wide_flux, (2,) + traces[1:], traces, full],
        partial, local, *incoming, flux_rows, near, orient, lift,
    )
    return jnp.transpose(final, (1, 0, 2))[None]


def solution(mesh):
    in_specs = (
        P(("group", "dom"), None, None, None),
        P(("group", "dom"), None, None),
        P(("group", "dom"), None),
        P(),
        P(),
        P(),
        P(),
        P(),
        P(),
        P(),
        P(None, ("group", "dom"), None),
        P(None, ("group", "dom"), None, None),
        P(None, ("group", "dom"), None),
        P(("group", "dom"), None),
        P("group", None),
    )
    out_specs = P(("group", "dom"), None, None, None)
    return jax.shard_map(shards, mesh=mesh, in_specs=in_specs, out_specs=out_specs, check_vma=False)
```

```python
import functools

import jax
import jax.numpy as jnp
from jax import lax
from jax.experimental import pallas as pl
from jax.experimental.pallas import tpu as pltpu
from jax.sharding import PartitionSpec as P

TAYLOR = 6
FIELDS = 9
LANES = 128
FACE_PAD = 24
TRACE_ROWS = FIELDS * FACE_PAD
MSG_ROWS = 112
LATER = 7
COEF_PAD = 16
STAR_ROWS = 27 * COEF_PAD
FLUX_ROWS = 18 * COEF_PAD
VALUES = 512

highest = lax.Precision.HIGHEST
friction_coef = 0.6
relax_share = 0.5
f32 = jnp.float32
bf16 = jnp.bfloat16


def halves(x):
    hi = x.astype(bf16)
    return hi, (x - hi.astype(f32)).astype(bf16)


def left_matrix(a):
    hi, lo = halves(a)
    both = jnp.concatenate([hi.astype(f32), lo.astype(f32)], axis=0).astype(bf16)
    return both, hi


def mm(left, x):
    both, hi = left
    x_hi, x_lo = halves(x)
    rows = hi.shape[0]
    first = jnp.dot(both, x_hi, preferred_element_type=f32)
    return first[:rows] + (first[rows:] + jnp.dot(hi, x_lo, preferred_element_type=f32))


def lane_gather(x, lane):
    return jnp.take_along_axis(x, jnp.broadcast_to(lane, x.shape), axis=1, mode="promise_in_bounds")


def choose(traces, index):
    rows, size = traces.shape
    wide = (size, index.shape[1])
    hot = (lax.broadcasted_iota(jnp.int32, wide, 0) == index).astype(bf16)
    hi, lo = halves(traces)
    return jnp.dot(hi, hot, preferred_element_type=f32) + jnp.dot(
        lo, hot, preferred_element_type=f32
    )


def block(f):
    return slice(f * LANES, (f + 1) * LANES)


def exact_dot(a, hot):
    total = None
    for _ in range(3):
        part = a.astype(bf16)
        a = a - part.astype(f32)
        term = jnp.dot(part, hot, preferred_element_type=f32)
        total = term if total is None else total + term
    return total


def coefficient_rows(table, hot):
    count = table.shape[0] // 8
    size = -(-table.shape[0] // LANES) * LANES
    wide = jnp.concatenate([table, jnp.zeros((table.shape[0], LANES - FIELDS), f32)], axis=1)
    if size > table.shape[0]:
        wide = jnp.concatenate([wide, jnp.zeros((size - table.shape[0], LANES), f32)], axis=0)
    turned = jnp.transpose(wide, (1, 0))[:COEF_PAD]
    stacked = jnp.concatenate([turned] * count, axis=0)
    pair = lax.broadcasted_iota(jnp.int32, stacked.shape, 0) // COEF_PAD
    at = lax.broadcasted_iota(jnp.int32, stacked.shape, 1) // 8
    many = jnp.concatenate([hot] * (size // 8), axis=0).astype(bf16)
    return exact_dot(jnp.where(pair == at, stacked, 0.0), many)


def mix(load, rows_ref, start, outs):
    accs = [None] * len(outs)
    for f in range(FIELDS):
        value = load(f)
        rows = value.shape[0]
        value = value.reshape(rows // 8, 8, LANES)
        for t, g in enumerate(outs):
            r = (start // FIELDS + f) * COEF_PAD + g
            part = value * jnp.broadcast_to(rows_ref[r : r + 1, :], (8, LANES))[None]
            accs[t] = part if accs[t] is None else accs[t] + part
    return [a.reshape(-1, LANES) for a in accs]


GROUPS_OF_FIELDS = ((0, 1), (2, 3), (4, 5), (6, 7), (8,))


def star_mixed(src_ref, rows_ref, outs):
    load = lambda f: src_ref[:, block(f)]
    parts = []
    for d in range(3):
        parts.append(jnp.concatenate(mix(load, rows_ref, d * 81, outs), axis=1))
    return jnp.concatenate(parts, axis=0)


def fetch(pairs, sems):
    copies = [pltpu.make_async_copy(a, b, sems.at[n]) for n, (a, b) in enumerate(pairs)]
    for copy in copies:
        copy.start()
    return copies


def one_hot(desc):
    kinds = lax.broadcasted_iota(jnp.int32, (8, LANES), 0).astype(f32)
    return (jnp.broadcast_to(desc[3:4], (8, LANES)) == kinds).astype(f32)


def first_half_body(place, refs):
    phase = 1 if place else 0
    if place:
        (state_ref, recv_ref, maps_ref, desc_ref, star_ref, send_ref, stiff_ref, project_ref,
         integral_ref, trace_ref, m0, m1, m2, m3, ops_ref, hot_ref, placed_ref,
         deriv_ref, padded_ref) = refs
    else:
        count = 7 + LATER
        inputs, refs = refs[:count], refs[count:]
        (integral_ref, trace_ref, m0, m1, m2, m3, ops_ref, hot_ref, desc_ref) = refs[:9]
        held = refs[9 : 14 + LATER]
        state_ref, star_ref, send_ref, stiff_ref, project_ref = held[:5]
        (deriv_ref, padded_ref, geometry_ref, material_ref, sems) = refs[14 + LATER :]
        targets = [geometry_ref, material_ref] + list(held)
        copies = fetch(list(zip(inputs, targets)), sems)
        for copy in copies[:7]:
            copy.wait()
        desc_ref[...] = jnp.zeros((8, LANES), f32)
        for d in range(3):
            desc_ref[d : d + 1, :] = geometry_ref[d]
        desc_ref[3:4, :] = material_ref[...].astype(f32)
    modes = stiff_ref.shape[1]

    desc = desc_ref[...]
    if place:
        arriving = maps_ref[1:2, :]
        arrives = arriving >= 0
        lane = jnp.maximum(arriving, 0)
        moved = []
        for b in range(4):
            got = recv_ref[pl.ds(b, 64, stride=4), :]
            got = jnp.concatenate([got, got], axis=0)
            moved.append(lane_gather(jnp.transpose(got, (1, 0)), lane))
        moved = jnp.concatenate(moved, axis=0)
        for f in range(FIELDS):
            new = jnp.where(arrives, moved[f * modes : (f + 1) * modes], state_ref[:, block(f)])
            placed_ref[:, block(f)] = new
        desc = jnp.where(arrives, moved[FIELDS * modes :], desc)
        integral_ref[...] = placed_ref[...]
    else:
        for f in range(FIELDS):
            integral_ref[:, block(f)] = state_ref[f]

    hot = one_hot(desc)
    hot_ref[...] = hot
    rows = coefficient_rows(star_ref[...], hot)
    row_at = lax.broadcasted_iota(jnp.int32, (STAR_ROWS, LANES), 0)
    third = STAR_ROWS // 3
    scale = jnp.where(row_at < third, desc[0:1], jnp.where(row_at < 2 * third, desc[1:2], desc[2:3]))
    ops_ref[...] = rows * scale
    across = jnp.concatenate([jnp.transpose(stiff_ref[d], (1, 0)) for d in range(3)], axis=0)
    stiff = left_matrix(-jnp.transpose(across, (1, 0)))
    deriv_ref[0] = integral_ref[...]

    def degree(j, coef):
        now = deriv_ref.at[j % 2]
        later = deriv_ref.at[(j + 1) % 2]
        for outs in GROUPS_OF_FIELDS:
            new = mm(stiff, star_mixed(now, ops_ref, outs))
            lanes = slice(outs[0] * LANES, (outs[-1] + 1) * LANES)
            later[:, lanes] = new
            integral_ref[:, lanes] = integral_ref[:, lanes] + new * coef

    coef = 1.0
    for j in range(TAYLOR - 1):
        coef = coef / (j + 2)
        degree(j, coef)

    padded_ref[...] = jnp.zeros(padded_ref.shape, f32)
    for i in range(4):
        padded_ref[i * FACE_PAD : i * FACE_PAD + project_ref.shape[0], :] = project_ref[:, i, :]
    project = left_matrix(padded_ref[...])
    for outs in GROUPS_OF_FIELDS:
        lanes = slice(outs[0] * LANES, (outs[-1] + 1) * LANES)
        traced = mm(project, integral_ref[:, lanes])
        for t, f in enumerate(outs):
            for i in range(4):
                trace_ref[i, f * FACE_PAD : (f + 1) * FACE_PAD, :] = traced[
                    i * FACE_PAD : (i + 1) * FACE_PAD, block(t)
                ]

    traces = jnp.concatenate([trace_ref[i] for i in range(4)], axis=1)
    low = lax.broadcasted_iota(jnp.int32, (MSG_ROWS, LANES), 1) < 64
    fill = jnp.zeros((2 * MSG_ROWS - TRACE_ROWS, LANES), f32)
    for k, (a, b) in enumerate(((m0, m1), (m2, m3))):
        pair = [send_ref[phase, 0, c : c + 1, :] for c in (2 * k, 2 * k + 1)]
        sent = choose(traces, jnp.concatenate(pair, axis=1))
        upper = jnp.concatenate([sent[MSG_ROWS:], fill], axis=0)
        a[...] = jnp.where(low, sent[:MSG_ROWS], pltpu.roll(upper, 64, 1))
        b[...] = jnp.where(low, pltpu.roll(sent[:MSG_ROWS], 64, 1), upper)
    if not place:
        for copy in copies[7:]:
            copy.wait()


def to_column(row, size):
    square = (size, row.shape[1])
    diagonal = lax.broadcasted_iota(jnp.int32, square, 0) == lax.broadcasted_iota(
        jnp.int32, square, 1
    )
    return jnp.sum(jnp.where(diagonal, row, 0.0), axis=1, keepdims=True)


def migration_maps(slots, owners, my_dom):
    doms, leave = owners.shape
    capacity = 2 * leave // doms
    total = capacity * doms
    iota = lambda shape, dim: lax.broadcasted_iota(jnp.int32, shape, dim)
    owner = jnp.sum(
        jnp.where(iota(owners.shape, 0) == my_dom, owners, 0).astype(f32), axis=0, keepdims=True
    )
    owner_col = to_column(owner, leave)
    slots_col = to_column(slots.astype(f32), leave)
    square = (leave, leave)
    before = (owner == owner_col) & (iota(square, 1) < iota(square, 0))
    rank = jnp.sum(jnp.where(before, 1.0, 0.0), axis=1, keepdims=True)
    send_slot = owner_col * capacity + rank
    wide = (leave, LANES)
    slot = (iota(wide, 1) % total).astype(f32)
    source = jnp.sum(jnp.where(send_slot == slot, slots_col, 0.0), axis=0, keepdims=True)

    arrivals = jnp.sum(jnp.where(owners == my_dom, 1.0, 0.0), axis=1, keepdims=True)
    wide = (doms, LANES)
    sender = iota(wide, 1) // capacity
    mine = jnp.sum(jnp.where(iota(wide, 0) == sender, arrivals, 0.0), axis=0, keepdims=True)
    ahead = jnp.sum(jnp.where(iota(wide, 0) < sender, arrivals, 0.0), axis=0, keepdims=True)
    lane = iota((1, LANES), 1)
    within = (lane % capacity).astype(f32)
    position = jnp.where((lane < total) & (within < mine), ahead + within, -1.0)
    position_col = to_column(position, LANES)
    wide = (leave, LANES)
    here = slots_col == iota(wide, 1).astype(f32)
    order = iota(wide, 0).astype(f32) + 1.0
    number = jnp.sum(jnp.where(here, order, 0.0), axis=0, keepdims=True) - 1.0
    wide = (LANES, LANES)
    hit = (position_col == number) & (jnp.broadcast_to(number, wide) >= 0.0)
    arriving = jnp.sum(
        jnp.where(hit, iota(wide, 0).astype(f32) + 1.0, 0.0), axis=0, keepdims=True
    )
    return source.astype(jnp.int32), arriving.astype(jnp.int32) - 1


def middle_body(phase, refs):
    (state_ref, integral_ref, trace_ref, ops_ref, hot_ref, near_ref, _, stiff_ref, flux_ref,
     cohesion_ref) = refs[:10]
    if phase == 0:
        (lift_in, project_ref, reorient_ref, slots_ref, owners_ref,
         partial_ref, local_ref, flux_rows_ref, own_ref, lift_ref, maps_ref,
         columns_ref) = refs[10:]
        own_ref[...] = sum(
            jnp.dot(
                jnp.transpose(lift_in[:, i, :], (1, 0)), project_ref[:, i, :],
                precision=highest, preferred_element_type=f32,
            )
            for i in range(4)
        )
        columns_ref[...] = jnp.zeros(columns_ref.shape, f32)
        face_modes = reorient_ref.shape[1]
        for h in range(3):
            back = jnp.transpose(reorient_ref[h], (1, 0))
            for i in range(4):
                at = (i * 3 + h) * FACE_PAD
                columns_ref[at : at + face_modes, :] = jnp.dot(
                    back, lift_in[:, i, :], precision=highest, preferred_element_type=f32
                )
        lift_ref[...] = jnp.transpose(columns_ref[...], (1, 0))
        source, arriving = migration_maps(slots_ref[...], owners_ref[...], lax.axis_index("dom"))
        maps_ref[0:1, :] = source
        maps_ref[1:2, :] = arriving
    else:
        own_ref, partial_ref, local_ref, flux_rows_ref = refs[10:]
    modes = stiff_ref.shape[1]
    hot = hot_ref[...]
    flux_rows_ref[0:FLUX_ROWS, :] = coefficient_rows(flux_ref[...], hot)
    yield_rows = exact_dot(jnp.broadcast_to(cohesion_ref[...], (8, 8)), hot.astype(bf16))
    flux_rows_ref[FLUX_ROWS : FLUX_ROWS + 8, :] = yield_rows
    volume = left_matrix(jnp.transpose(stiff_ref[...].reshape(3 * modes, modes), (1, 0)))
    own = left_matrix(own_ref[...])
    for outs in GROUPS_OF_FIELDS:
        lanes = slice(outs[0] * LANES, (outs[-1] + 1) * LANES)
        load = lambda f: integral_ref[:, block(f)]
        added = mm(volume, star_mixed(integral_ref, ops_ref, outs))
        flux = mm(own, jnp.concatenate(mix(load, flux_rows_ref, 0, outs), axis=1))
        if len(state_ref.shape) == 3:
            before = jnp.concatenate([state_ref[g] for g in outs], axis=1)
        else:
            before = state_ref[:, lanes]
        partial_ref[:, lanes] = before + added - flux
    for i in range(4):
        index = jnp.broadcast_to(near_ref[phase, :, block(i)], (8, LANES))
        lane, source = index & 127, index >> 7
        for r in range(TRACE_ROWS // 8):
            rows = slice(r * 8, r * 8 + 8)
            out = None
            for j in range(4):
                got = lane_gather(trace_ref[j, rows, :], lane)
                out = got if out is None else jnp.where(source == j, got, out)
            local_ref[i, rows, :] = out


def last_half_body(pack, refs):
    phase = 0 if pack else 1
    if pack:
        (partial_ref, local_ref, m0, m1, m2, m3, ops_ref, near_ref, orient_ref, lift_ref,
         desc_ref, maps_ref, out_ref, packed_ref, both_ref, turned_ref, sum_ref) = refs
    else:
        (partial_ref, local_ref, m0, m1, m2, m3, ops_ref, near_ref, orient_ref, lift_ref,
         out_ref, both_ref, turned_ref, sum_ref) = refs
    modes = lift_ref.shape[0]

    low = lax.broadcasted_iota(jnp.int32, (MSG_ROWS, LANES), 1) < 64
    rest = TRACE_ROWS - MSG_ROWS
    for k, (a, b) in enumerate(((m0, m1), (m2, m3))):
        first, second = a[...], b[...]
        both_ref[k, 0:MSG_ROWS, :] = jnp.where(low, first, pltpu.roll(second, 64, 1))
        upper = jnp.where(low, pltpu.roll(first, 64, 1), second)
        both_ref[k, MSG_ROWS:TRACE_ROWS, :] = upper[:rest]

    for i in range(4):
        index = jnp.broadcast_to(near_ref[phase, :, block(i)], (8, LANES))
        lane, source = index & 127, index >> 7
        for r in range(TRACE_ROWS // 8):
            rows = slice(r * 8, r * 8 + 8)
            out = local_ref[i, rows, :]
            for k in range(2):
                out = jnp.where(source == 4 + k, lane_gather(both_ref[k, rows, :], lane), out)
            turned_ref[i, rows, :] = out

    lift = left_matrix(lift_ref[...])
    for outs in GROUPS_OF_FIELDS:
        lanes = slice(outs[0] * LANES, (outs[-1] + 1) * LANES)
        pieces = []
        for i in range(4):
            load = lambda f: turned_ref[i, f * FACE_PAD : (f + 1) * FACE_PAD, :]
            mixed = mix(load, ops_ref, 81, outs)
            orient = jnp.broadcast_to(orient_ref[phase, :, block(i)], (FACE_PAD, LANES))
            for h in range(3):
                pieces.append(
                    jnp.concatenate([jnp.where(orient == h, m, 0.0) for m in mixed], axis=1)
                )
        flux = mm(lift, jnp.concatenate(pieces, axis=0))
        wide_out = partial_ref[:, lanes] - flux
        for t, g in enumerate(outs):
            sum_ref[:, block(g)] = wide_out[:, block(t)]

    zero = [sum_ref[0:1, block(f)] for f in range(6)]
    pressure_zero = -(zero[0] + zero[1] + zero[2]) / 3.0
    second = 0.5 * sum((zero[f] + pressure_zero) * (zero[f] + pressure_zero) for f in range(3))
    second = second + sum(zero[f] * zero[f] for f in range(3, 6))
    shear_mag = jnp.sqrt(second)
    yield_row = ops_ref[FLUX_ROWS : FLUX_ROWS + 1, :]
    yield_stress = yield_row + friction_coef * jnp.maximum(pressure_zero, 0.0)
    factor = 1.0 - relax_share * jnp.maximum(
        0.0, 1.0 - yield_stress / jnp.maximum(shear_mag, yield_stress)
    )
    normals = [sum_ref[:, block(f)] for f in range(3)]
    pressure = -(normals[0] + normals[1] + normals[2]) / 3.0
    fields = [-pressure + factor * (n + pressure) for n in normals]
    fields += [factor * sum_ref[:, block(f)] for f in range(3, 6)]
    fields += [sum_ref[:, block(f)] for f in range(6, FIELDS)]
    if not pack:
        for f in range(FIELDS):
            out_ref[f] = fields[f]
        return
    for f in range(FIELDS):
        out_ref[:, block(f)] = fields[f]
    values = jnp.concatenate(fields + [desc_ref[...]], axis=0)
    leaving = lane_gather(values, maps_ref[0:1, :])
    for b in range(4):
        turned = jnp.transpose(leaving[b * LANES : (b + 1) * LANES], (1, 0))
        packed_ref[pl.ds(b, 64, stride=4), :] = turned[:64]


def call(body, outs, scratch, *args, raw=False):
    space = pltpu.HBM if raw else pltpu.VMEM
    scratch = [s if not isinstance(s, tuple) else pltpu.VMEM(s, f32) for s in scratch]
    outs = [s if isinstance(s, jax.ShapeDtypeStruct) else jax.ShapeDtypeStruct(s, f32) for s in outs]
    return pl.pallas_call(
        lambda *refs: body(refs),
        out_shape=outs,
        in_specs=[pl.BlockSpec(memory_space=space)] * len(args),
        out_specs=[pl.BlockSpec(memory_space=pltpu.VMEM)] * len(outs),
        scratch_shapes=scratch,
        compiler_params=pltpu.CompilerParams(vmem_limit_bytes=48 << 20),
    )(*[pltpu.with_memory_space_constraint(a, pltpu.HBM) for a in args] if raw else args)


def exchange(messages):
    out = []
    for axis, (lower, higher) in (("group", messages[:2]), ("dom", messages[2:])):
        size = lax.axis_size(axis)
        up = [(i, (i + 1) % size) for i in range(size)]
        down = [(j, i) for i, j in up]
        out += [lax.ppermute(higher, axis, up), lax.ppermute(lower, axis, down)]
    return out


def shards(
    modal_state,
    geometry,
    material,
    star_table,
    flux_table,
    cohesion,
    stiffness,
    face_project,
    face_lift,
    reorient,
    neighbour_face,
    send_faces,
    orientation,
    leaving_slots,
    leaving_owner,
):
    modes, nfield, elem_count = modal_state.shape[1:]
    kinds = star_table.shape[0]
    state = jnp.transpose(modal_state[0], (1, 0, 2))
    star = jnp.transpose(star_table, (1, 2, 0, 3)).reshape(3 * nfield * kinds, nfield)
    flux = jnp.transpose(flux_table, (1, 2, 0, 3)).reshape(2 * nfield * kinds, nfield)
    cohesion = cohesion[None, :]
    geometry = jnp.transpose(geometry, (1, 0, 2))
    face_project = jnp.transpose(face_project, (1, 0, 2))
    face_lift = jnp.transpose(face_lift, (2, 0, 1))

    full = (modes, nfield * elem_count)
    traces = (4, TRACE_ROWS, LANES)
    msg = (MSG_ROWS, LANES)
    tile = (8, LANES)
    ops_shape = (STAR_ROWS, LANES)
    flux_shape = (FLUX_ROWS + 8, LANES)
    lift_shape = (modes, 12 * FACE_PAD)
    maps_shape = jax.ShapeDtypeStruct((2, LANES), jnp.int32)
    first_scratch = [(2,) + full, (4 * FACE_PAD, modes)]

    kept = [state, star, send_faces, stiffness, face_project,
            face_lift, reorient, leaving_slots, leaving_owner, neighbour_face, orientation, cohesion]
    (integral, trace, a, b, c, d, ops, hot, desc,
     state, star, sends, stiff, project, *later) = call(
        functools.partial(first_half_body, False),
        [full, traces, msg, msg, msg, msg, ops_shape, tile, tile]
        + [jax.ShapeDtypeStruct(a.shape, a.dtype) for a in kept],
        first_scratch
        + [pltpu.VMEM(geometry.shape, f32), pltpu.VMEM(material.shape, jnp.int32),
           pltpu.SemaphoreType.DMA((2 + len(kept),))],
        geometry, material, *kept,
        raw=True,
    )
    face_lift, reorient, slots, owners, near, orient, cohesion = later
    incoming = exchange([a, b, c, d])
    partial, local, flux_rows, own, lift, maps = call(
        functools.partial(middle_body, 0),
        [full, traces, flux_shape, (modes, modes), lift_shape, maps_shape],
        [(12 * FACE_PAD, modes)],
        state, integral, trace, ops, hot, near, orient, stiff, flux, cohesion,
        face_lift, project, reorient, slots, owners,
    )
    stepped, packed = call(
        functools.partial(last_half_body, True),
        [full, (256, LANES)],
        [(2,) + traces[1:], traces, full],
        partial, local, *incoming, flux_rows, near, orient, lift, desc, maps,
    )
    moved = lax.all_to_all(packed, "dom", split_axis=0, concat_axis=0, tiled=True)
    integral, trace, a, b, c, d, ops, hot, placed = call(
        functools.partial(first_half_body, True),
        [full, traces, msg, msg, msg, msg, ops_shape, tile, full],
        first_scratch,
        stepped, moved, maps, desc, star, sends, stiff, project,
    )
    incoming = exchange([a, b, c, d])
    partial, local, flux_rows = call(
        functools.partial(middle_body, 1),
        [full, traces, flux_shape],
        [],
        placed, integral, trace, ops, hot, near, orient, stiff, flux,
        cohesion, own,
    )
    (final,) = call(
        functools.partial(last_half_body, False),
        [(nfield, modes, elem_count)],
        [(2,) + traces[1:], traces, full],
        partial, local, *incoming, flux_rows, near, orient, lift,
    )
    return jnp.transpose(final, (1, 0, 2))[None]


def solution(mesh):
    in_specs = (
        P(("group", "dom"), None, None, None),
        P(("group", "dom"), None, None),
        P(("group", "dom"), None),
        P(),
        P(),
        P(),
        P(),
        P(),
        P(),
        P(),
        P(None, ("group", "dom"), None),
        P(None, ("group", "dom"), None, None),
        P(None, ("group", "dom"), None),
        P(("group", "dom"), None),
        P("group", None),
    )
    out_specs = P(("group", "dom"), None, None, None)
    return jax.shard_map(shards, mesh=mesh, in_specs=in_specs, out_specs=out_specs, check_vma=False)
```

```python
import functools

import jax
import jax.numpy as jnp
from jax import lax
from jax.experimental import pallas as pl
from jax.experimental.pallas import tpu as pltpu
from jax.sharding import PartitionSpec as P

TAYLOR = 6
FIELDS = 9
LANES = 128
FACE_PAD = 24
TRACE_ROWS = FIELDS * FACE_PAD
MSG_ROWS = 112
LATER = 7
COEF_PAD = 16
STAR_ROWS = 27 * COEF_PAD
FLUX_ROWS = 18 * COEF_PAD
VALUES = 512

highest = lax.Precision.HIGHEST
friction_coef = 0.6
relax_share = 0.5
f32 = jnp.float32
bf16 = jnp.bfloat16


def halves(x):
    hi = x.astype(bf16)
    return hi, (x - hi.astype(f32)).astype(bf16)


def left_matrix(a):
    hi, lo = halves(a)
    both = jnp.concatenate([hi.astype(f32), lo.astype(f32)], axis=0).astype(bf16)
    return both, hi


def mm(left, x):
    both, hi = left
    x_hi, x_lo = halves(x)
    rows = hi.shape[0]
    first = jnp.dot(both, x_hi, preferred_element_type=f32)
    return first[:rows] + (first[rows:] + jnp.dot(hi, x_lo, preferred_element_type=f32))


def lane_gather(x, lane):
    return jnp.take_along_axis(x, jnp.broadcast_to(lane, x.shape), axis=1, mode="promise_in_bounds")


def choose(traces, index):
    rows, size = traces.shape
    wide = (size, index.shape[1])
    hot = (lax.broadcasted_iota(jnp.int32, wide, 0) == index).astype(bf16)
    hi, lo = halves(traces)
    return jnp.dot(hi, hot, preferred_element_type=f32) + jnp.dot(
        lo, hot, preferred_element_type=f32
    )


def block(f):
    return slice(f * LANES, (f + 1) * LANES)


def exact_dot(a, hot):
    total = None
    for _ in range(3):
        part = a.astype(bf16)
        a = a - part.astype(f32)
        term = jnp.dot(part, hot, preferred_element_type=f32)
        total = term if total is None else total + term
    return total


def coefficient_rows(table, hot):
    count = table.shape[0] // 8
    size = -(-table.shape[0] // LANES) * LANES
    wide = jnp.concatenate([table, jnp.zeros((table.shape[0], LANES - FIELDS), f32)], axis=1)
    if size > table.shape[0]:
        wide = jnp.concatenate([wide, jnp.zeros((size - table.shape[0], LANES), f32)], axis=0)
    turned = jnp.transpose(wide, (1, 0))[:COEF_PAD]
    stacked = jnp.concatenate([turned] * count, axis=0)
    pair = lax.broadcasted_iota(jnp.int32, stacked.shape, 0) // COEF_PAD
    at = lax.broadcasted_iota(jnp.int32, stacked.shape, 1) // 8
    many = jnp.concatenate([hot] * (size // 8), axis=0).astype(bf16)
    return exact_dot(jnp.where(pair == at, stacked, 0.0), many)


def spread_rows(ops_ref, first, count, wide_ref, start=0):
    for p in range(count):
        for g in range(FIELDS):
            r = (first + p) * COEF_PAD + g
            wide_ref[start + p * FIELDS + g] = jnp.broadcast_to(ops_ref[r : r + 1, :], (8, LANES))


def mix(load, wide_ref, start, outs):
    accs = [None] * len(outs)
    for f in range(FIELDS):
        value = load(f)
        rows = value.shape[0]
        value = value.reshape(rows // 8, 8, LANES)
        for t, g in enumerate(outs):
            part = value * wide_ref[start + f * FIELDS + g][None]
            accs[t] = part if accs[t] is None else accs[t] + part
    return [a.reshape(-1, LANES) for a in accs]


GROUPS_OF_FIELDS = ((0, 1), (2, 3), (4, 5), (6, 7), (8,))


def star_mixed(src_ref, wide_ref, outs):
    load = lambda f: src_ref[:, block(f)]
    parts = []
    for d in range(3):
        parts.append(jnp.concatenate(mix(load, wide_ref, d * 81, outs), axis=1))
    return jnp.concatenate(parts, axis=0)


def fetch(pairs, sems):
    copies = [pltpu.make_async_copy(a, b, sems.at[n]) for n, (a, b) in enumerate(pairs)]
    for copy in copies:
        copy.start()
    return copies


def one_hot(desc):
    kinds = lax.broadcasted_iota(jnp.int32, (8, LANES), 0).astype(f32)
    return (jnp.broadcast_to(desc[3:4], (8, LANES)) == kinds).astype(f32)


def first_half_body(place, refs):
    phase = 1 if place else 0
    if place:
        (state_ref, recv_ref, maps_ref, desc_ref, star_ref, send_ref, stiff_ref, project_ref,
         integral_ref, trace_ref, m0, m1, m2, m3, ops_ref, hot_ref, placed_ref,
         wide_ref, deriv_ref, padded_ref) = refs
    else:
        count = 7 + LATER
        inputs, refs = refs[:count], refs[count:]
        (integral_ref, trace_ref, m0, m1, m2, m3, ops_ref, hot_ref, desc_ref) = refs[:9]
        held = refs[9 : 14 + LATER]
        state_ref, star_ref, send_ref, stiff_ref, project_ref = held[:5]
        (wide_ref, deriv_ref, padded_ref, geometry_ref, material_ref, sems) = refs[14 + LATER :]
        targets = [geometry_ref, material_ref] + list(held)
        copies = fetch(list(zip(inputs, targets)), sems)
        for n in (0, 1, 3):
            copies[n].wait()
        desc_ref[...] = jnp.zeros((8, LANES), f32)
        for d in range(3):
            desc_ref[d : d + 1, :] = geometry_ref[d]
        desc_ref[3:4, :] = material_ref[...].astype(f32)
    modes = stiff_ref.shape[1]

    desc = desc_ref[...]
    if place:
        arriving = maps_ref[1:2, :]
        arrives = arriving >= 0
        lane = jnp.maximum(arriving, 0)
        moved = []
        for b in range(4):
            got = recv_ref[pl.ds(b, 64, stride=4), :]
            got = jnp.concatenate([got, got], axis=0)
            moved.append(lane_gather(jnp.transpose(got, (1, 0)), lane))
        moved = jnp.concatenate(moved, axis=0)
        for f in range(FIELDS):
            new = jnp.where(arrives, moved[f * modes : (f + 1) * modes], state_ref[:, block(f)])
            placed_ref[:, block(f)] = new
        desc = jnp.where(arrives, moved[FIELDS * modes :], desc)
        integral_ref[...] = placed_ref[...]

    hot = one_hot(desc)
    hot_ref[...] = hot
    rows = coefficient_rows(star_ref[...], hot)
    row_at = lax.broadcasted_iota(jnp.int32, (STAR_ROWS, LANES), 0)
    third = STAR_ROWS // 3
    scale = jnp.where(row_at < third, desc[0:1], jnp.where(row_at < 2 * third, desc[1:2], desc[2:3]))
    ops_ref[...] = rows * scale
    spread_rows(ops_ref, 0, 27, wide_ref)

    if not place:
        for n in (2, 4, 5, 6):
            copies[n].wait()
        for f in range(FIELDS):
            integral_ref[:, block(f)] = state_ref[f]

    across = jnp.concatenate([jnp.transpose(stiff_ref[d], (1, 0)) for d in range(3)], axis=0)
    stiff = left_matrix(-jnp.transpose(across, (1, 0)))
    deriv_ref[0] = integral_ref[...]

    def degree(j, coef):
        now = deriv_ref.at[j % 2]
        later = deriv_ref.at[(j + 1) % 2]
        for outs in GROUPS_OF_FIELDS:
            new = mm(stiff, star_mixed(now, wide_ref, outs))
            lanes = slice(outs[0] * LANES, (outs[-1] + 1) * LANES)
            later[:, lanes] = new
            integral_ref[:, lanes] = integral_ref[:, lanes] + new * coef

    coef = 1.0
    for j in range(TAYLOR - 1):
        coef = coef / (j + 2)
        degree(j, coef)

    padded_ref[...] = jnp.zeros(padded_ref.shape, f32)
    for i in range(4):
        padded_ref[i * FACE_PAD : i * FACE_PAD + project_ref.shape[0], :] = project_ref[:, i, :]
    project = left_matrix(padded_ref[...])
    for outs in GROUPS_OF_FIELDS:
        lanes = slice(outs[0] * LANES, (outs[-1] + 1) * LANES)
        traced = mm(project, integral_ref[:, lanes])
        for t, f in enumerate(outs):
            for i in range(4):
                trace_ref[i, f * FACE_PAD : (f + 1) * FACE_PAD, :] = traced[
                    i * FACE_PAD : (i + 1) * FACE_PAD, block(t)
                ]

    traces = jnp.concatenate([trace_ref[i] for i in range(4)], axis=1)
    low = lax.broadcasted_iota(jnp.int32, (MSG_ROWS, LANES), 1) < 64
    fill = jnp.zeros((2 * MSG_ROWS - TRACE_ROWS, LANES), f32)
    for k, (a, b) in enumerate(((m0, m1), (m2, m3))):
        pair = [send_ref[phase, 0, c : c + 1, :] for c in (2 * k, 2 * k + 1)]
        sent = choose(traces, jnp.concatenate(pair, axis=1))
        upper = jnp.concatenate([sent[MSG_ROWS:], fill], axis=0)
        a[...] = jnp.where(low, sent[:MSG_ROWS], pltpu.roll(upper, 64, 1))
        b[...] = jnp.where(low, pltpu.roll(sent[:MSG_ROWS], 64, 1), upper)
    if not place:
        for copy in copies[7:]:
            copy.wait()


def to_column(row, size):
    square = (size, row.shape[1])
    diagonal = lax.broadcasted_iota(jnp.int32, square, 0) == lax.broadcasted_iota(
        jnp.int32, square, 1
    )
    return jnp.sum(jnp.where(diagonal, row, 0.0), axis=1, keepdims=True)


def migration_maps(slots, owners, my_dom):
    doms, leave = owners.shape
    capacity = 2 * leave // doms
    total = capacity * doms
    iota = lambda shape, dim: lax.broadcasted_iota(jnp.int32, shape, dim)
    owner = jnp.sum(
        jnp.where(iota(owners.shape, 0) == my_dom, owners, 0).astype(f32), axis=0, keepdims=True
    )
    owner_col = to_column(owner, leave)
    slots_col = to_column(slots.astype(f32), leave)
    square = (leave, leave)
    before = (owner == owner_col) & (iota(square, 1) < iota(square, 0))
    rank = jnp.sum(jnp.where(before, 1.0, 0.0), axis=1, keepdims=True)
    send_slot = owner_col * capacity + rank
    wide = (leave, LANES)
    slot = (iota(wide, 1) % total).astype(f32)
    source = jnp.sum(jnp.where(send_slot == slot, slots_col, 0.0), axis=0, keepdims=True)

    arrivals = jnp.sum(jnp.where(owners == my_dom, 1.0, 0.0), axis=1, keepdims=True)
    wide = (doms, LANES)
    sender = iota(wide, 1) // capacity
    mine = jnp.sum(jnp.where(iota(wide, 0) == sender, arrivals, 0.0), axis=0, keepdims=True)
    ahead = jnp.sum(jnp.where(iota(wide, 0) < sender, arrivals, 0.0), axis=0, keepdims=True)
    lane = iota((1, LANES), 1)
    within = (lane % capacity).astype(f32)
    position = jnp.where((lane < total) & (within < mine), ahead + within, -1.0)
    position_col = to_column(position, LANES)
    wide = (leave, LANES)
    here = slots_col == iota(wide, 1).astype(f32)
    order = iota(wide, 0).astype(f32) + 1.0
    number = jnp.sum(jnp.where(here, order, 0.0), axis=0, keepdims=True) - 1.0
    wide = (LANES, LANES)
    hit = (position_col == number) & (jnp.broadcast_to(number, wide) >= 0.0)
    arriving = jnp.sum(
        jnp.where(hit, iota(wide, 0).astype(f32) + 1.0, 0.0), axis=0, keepdims=True
    )
    return source.astype(jnp.int32), arriving.astype(jnp.int32) - 1


def middle_body(phase, refs):
    (state_ref, integral_ref, trace_ref, ops_ref, hot_ref, near_ref, _, stiff_ref, flux_ref,
     cohesion_ref) = refs[:10]
    if phase == 0:
        (lift_in, project_ref, reorient_ref, slots_ref, owners_ref,
         partial_ref, local_ref, flux_rows_ref, own_ref, lift_ref, maps_ref,
         wide_ref, columns_ref) = refs[10:]
        own_ref[...] = sum(
            jnp.dot(
                jnp.transpose(lift_in[:, i, :], (1, 0)), project_ref[:, i, :],
                precision=highest, preferred_element_type=f32,
            )
            for i in range(4)
        )
        columns_ref[...] = jnp.zeros(columns_ref.shape, f32)
        face_modes = reorient_ref.shape[1]
        for h in range(3):
            back = jnp.transpose(reorient_ref[h], (1, 0))
            for i in range(4):
                at = (i * 3 + h) * FACE_PAD
                columns_ref[at : at + face_modes, :] = jnp.dot(
                    back, lift_in[:, i, :], precision=highest, preferred_element_type=f32
                )
        lift_ref[...] = jnp.transpose(columns_ref[...], (1, 0))
        source, arriving = migration_maps(slots_ref[...], owners_ref[...], lax.axis_index("dom"))
        maps_ref[0:1, :] = source
        maps_ref[1:2, :] = arriving
    else:
        own_ref, partial_ref, local_ref, flux_rows_ref, wide_ref = refs[10:]
    modes = stiff_ref.shape[1]
    hot = hot_ref[...]
    flux_rows_ref[0:FLUX_ROWS, :] = coefficient_rows(flux_ref[...], hot)
    yield_rows = exact_dot(jnp.broadcast_to(cohesion_ref[...], (8, 8)), hot.astype(bf16))
    flux_rows_ref[FLUX_ROWS : FLUX_ROWS + 8, :] = yield_rows
    spread_rows(ops_ref, 0, 27, wide_ref)
    spread_rows(flux_rows_ref, 0, 9, wide_ref, 243)
    volume = left_matrix(jnp.transpose(stiff_ref[...].reshape(3 * modes, modes), (1, 0)))
    own = left_matrix(own_ref[...])
    for outs in GROUPS_OF_FIELDS:
        lanes = slice(outs[0] * LANES, (outs[-1] + 1) * LANES)
        load = lambda f: integral_ref[:, block(f)]
        added = mm(volume, star_mixed(integral_ref, wide_ref, outs))
        flux = mm(own, jnp.concatenate(mix(load, wide_ref, 243, outs), axis=1))
        if len(state_ref.shape) == 3:
            before = jnp.concatenate([state_ref[g] for g in outs], axis=1)
        else:
            before = state_ref[:, lanes]
        partial_ref[:, lanes] = before + added - flux
    for i in range(4):
        index = jnp.broadcast_to(near_ref[phase, :, block(i)], (8, LANES))
        lane, source = index & 127, index >> 7
        for r in range(TRACE_ROWS // 8):
            rows = slice(r * 8, r * 8 + 8)
            out = None
            for j in range(4):
                got = lane_gather(trace_ref[j, rows, :], lane)
                out = got if out is None else jnp.where(source == j, got, out)
            local_ref[i, rows, :] = out


def last_half_body(pack, refs):
    phase = 0 if pack else 1
    if pack:
        (partial_ref, local_ref, m0, m1, m2, m3, ops_ref, near_ref, orient_ref, lift_ref,
         desc_ref, maps_ref, out_ref, packed_ref, wide_ref, both_ref, turned_ref, sum_ref) = refs
    else:
        (partial_ref, local_ref, m0, m1, m2, m3, ops_ref, near_ref, orient_ref, lift_ref,
         out_ref, wide_ref, both_ref, turned_ref, sum_ref) = refs
    modes = lift_ref.shape[0]
    spread_rows(ops_ref, 9, 9, wide_ref)

    low = lax.broadcasted_iota(jnp.int32, (MSG_ROWS, LANES), 1) < 64
    rest = TRACE_ROWS - MSG_ROWS
    for k, (a, b) in enumerate(((m0, m1), (m2, m3))):
        first, second = a[...], b[...]
        both_ref[k, 0:MSG_ROWS, :] = jnp.where(low, first, pltpu.roll(second, 64, 1))
        upper = jnp.where(low, pltpu.roll(first, 64, 1), second)
        both_ref[k, MSG_ROWS:TRACE_ROWS, :] = upper[:rest]

    for i in range(4):
        index = jnp.broadcast_to(near_ref[phase, :, block(i)], (8, LANES))
        lane, source = index & 127, index >> 7
        for r in range(TRACE_ROWS // 8):
            rows = slice(r * 8, r * 8 + 8)
            out = local_ref[i, rows, :]
            for k in range(2):
                out = jnp.where(source == 4 + k, lane_gather(both_ref[k, rows, :], lane), out)
            turned_ref[i, rows, :] = out

    lift = left_matrix(lift_ref[...])
    for outs in GROUPS_OF_FIELDS:
        lanes = slice(outs[0] * LANES, (outs[-1] + 1) * LANES)
        pieces = []
        for i in range(4):
            load = lambda f: turned_ref[i, f * FACE_PAD : (f + 1) * FACE_PAD, :]
            mixed = mix(load, wide_ref, 0, outs)
            orient = jnp.broadcast_to(orient_ref[phase, :, block(i)], (FACE_PAD, LANES))
            for h in range(3):
                pieces.append(
                    jnp.concatenate([jnp.where(orient == h, m, 0.0) for m in mixed], axis=1)
                )
        flux = mm(lift, jnp.concatenate(pieces, axis=0))
        wide_out = partial_ref[:, lanes] - flux
        for t, g in enumerate(outs):
            sum_ref[:, block(g)] = wide_out[:, block(t)]

    zero = [sum_ref[0:1, block(f)] for f in range(6)]
    pressure_zero = -(zero[0] + zero[1] + zero[2]) / 3.0
    second = 0.5 * sum((zero[f] + pressure_zero) * (zero[f] + pressure_zero) for f in range(3))
    second = second + sum(zero[f] * zero[f] for f in range(3, 6))
    shear_mag = jnp.sqrt(second)
    yield_row = ops_ref[FLUX_ROWS : FLUX_ROWS + 1, :]
    yield_stress = yield_row + friction_coef * jnp.maximum(pressure_zero, 0.0)
    factor = 1.0 - relax_share * jnp.maximum(
        0.0, 1.0 - yield_stress / jnp.maximum(shear_mag, yield_stress)
    )
    normals = [sum_ref[:, block(f)] for f in range(3)]
    pressure = -(normals[0] + normals[1] + normals[2]) / 3.0
    fields = [-pressure + factor * (n + pressure) for n in normals]
    fields += [factor * sum_ref[:, block(f)] for f in range(3, 6)]
    fields += [sum_ref[:, block(f)] for f in range(6, FIELDS)]
    if not pack:
        for f in range(FIELDS):
            out_ref[f] = fields[f]
        return
    for f in range(FIELDS):
        out_ref[:, block(f)] = fields[f]
    values = jnp.concatenate(fields + [desc_ref[...]], axis=0)
    leaving = lane_gather(values, maps_ref[0:1, :])
    for b in range(4):
        turned = jnp.transpose(leaving[b * LANES : (b + 1) * LANES], (1, 0))
        packed_ref[pl.ds(b, 64, stride=4), :] = turned[:64]


def call(body, outs, scratch, *args, raw=False):
    space = pltpu.HBM if raw else pltpu.VMEM
    scratch = [s if not isinstance(s, tuple) else pltpu.VMEM(s, f32) for s in scratch]
    outs = [s if isinstance(s, jax.ShapeDtypeStruct) else jax.ShapeDtypeStruct(s, f32) for s in outs]
    return pl.pallas_call(
        lambda *refs: body(refs),
        out_shape=outs,
        in_specs=[pl.BlockSpec(memory_space=space)] * len(args),
        out_specs=[pl.BlockSpec(memory_space=pltpu.VMEM)] * len(outs),
        scratch_shapes=scratch,
        compiler_params=pltpu.CompilerParams(vmem_limit_bytes=48 << 20),
    )(*[pltpu.with_memory_space_constraint(a, pltpu.HBM) for a in args] if raw else args)


def exchange(messages):
    out = []
    for axis, (lower, higher) in (("group", messages[:2]), ("dom", messages[2:])):
        size = lax.axis_size(axis)
        up = [(i, (i + 1) % size) for i in range(size)]
        down = [(j, i) for i, j in up]
        out += [lax.ppermute(higher, axis, up), lax.ppermute(lower, axis, down)]
    return out


def shards(
    modal_state,
    geometry,
    material,
    star_table,
    flux_table,
    cohesion,
    stiffness,
    face_project,
    face_lift,
    reorient,
    neighbour_face,
    send_faces,
    orientation,
    leaving_slots,
    leaving_owner,
):
    modes, nfield, elem_count = modal_state.shape[1:]
    kinds = star_table.shape[0]
    state = jnp.transpose(modal_state[0], (1, 0, 2))
    star = jnp.transpose(star_table, (1, 2, 0, 3)).reshape(3 * nfield * kinds, nfield)
    flux = jnp.transpose(flux_table, (1, 2, 0, 3)).reshape(2 * nfield * kinds, nfield)
    cohesion = cohesion[None, :]
    geometry = jnp.transpose(geometry, (1, 0, 2))
    face_project = jnp.transpose(face_project, (1, 0, 2))
    face_lift = jnp.transpose(face_lift, (2, 0, 1))

    full = (modes, nfield * elem_count)
    traces = (4, TRACE_ROWS, LANES)
    msg = (MSG_ROWS, LANES)
    tile = (8, LANES)
    ops_shape = (STAR_ROWS, LANES)
    flux_shape = (FLUX_ROWS + 8, LANES)
    wide = (243, 8, LANES)
    wide_more = (324, 8, LANES)
    wide_flux = (81, 8, LANES)
    lift_shape = (modes, 12 * FACE_PAD)
    maps_shape = jax.ShapeDtypeStruct((2, LANES), jnp.int32)
    first_scratch = [wide, (2,) + full, (4 * FACE_PAD, modes)]

    kept = [state, star, send_faces, stiffness, face_project,
            face_lift, reorient, leaving_slots, leaving_owner, neighbour_face, orientation, cohesion]
    (integral, trace, a, b, c, d, ops, hot, desc,
     state, star, sends, stiff, project, *later) = call(
        functools.partial(first_half_body, False),
        [full, traces, msg, msg, msg, msg, ops_shape, tile, tile]
        + [jax.ShapeDtypeStruct(a.shape, a.dtype) for a in kept],
        first_scratch
        + [pltpu.VMEM(geometry.shape, f32), pltpu.VMEM(material.shape, jnp.int32),
           pltpu.SemaphoreType.DMA((2 + len(kept),))],
        geometry, material, *kept,
        raw=True,
    )
    face_lift, reorient, slots, owners, near, orient, cohesion = later
    incoming = exchange([a, b, c, d])
    partial, local, flux_rows, own, lift, maps = call(
        functools.partial(middle_body, 0),
        [full, traces, flux_shape, (modes, modes), lift_shape, maps_shape],
        [wide_more, (12 * FACE_PAD, modes)],
        state, integral, trace, ops, hot, near, orient, stiff, flux, cohesion,
        face_lift, project, reorient, slots, owners,
    )
    stepped, packed = call(
        functools.partial(last_half_body, True),
        [full, (256, LANES)],
        [wide_flux, (2,) + traces[1:], traces, full],
        partial, local, *incoming, flux_rows, near, orient, lift, desc, maps,
    )
    moved = lax.all_to_all(packed, "dom", split_axis=0, concat_axis=0, tiled=True)
    integral, trace, a, b, c, d, ops, hot, placed = call(
        functools.partial(first_half_body, True),
        [full, traces, msg, msg, msg, msg, ops_shape, tile, full],
        first_scratch,
        stepped, moved, maps, desc, star, sends, stiff, project,
    )
    incoming = exchange([a, b, c, d])
    partial, local, flux_rows = call(
        functools.partial(middle_body, 1),
        [full, traces, flux_shape],
        [wide_more],
        placed, integral, trace, ops, hot, near, orient, stiff, flux,
        cohesion, own,
    )
    (final,) = call(
        functools.partial(last_half_body, False),
        [(nfield, modes, elem_count)],
        [wide_flux, (2,) + traces[1:], traces, full],
        partial, local, *incoming, flux_rows, near, orient, lift,
    )
    return jnp.transpose(final, (1, 0, 2))[None]


def solution(mesh):
    in_specs = (
        P(("group", "dom"), None, None, None),
        P(("group", "dom"), None, None),
        P(("group", "dom"), None),
        P(),
        P(),
        P(),
        P(),
        P(),
        P(),
        P(),
        P(None, ("group", "dom"), None),
        P(None, ("group", "dom"), None, None),
        P(None, ("group", "dom"), None),
        P(("group", "dom"), None),
        P("group", None),
    )
    out_specs = P(("group", "dom"), None, None, None)
    return jax.shard_map(shards, mesh=mesh, in_specs=in_specs, out_specs=out_specs, check_vma=False)
```
